768 devices in a mesh: dom: 96 (over z, y), sub: 8 (over x, core).
Axes of the slice: x: 4, y: 8, z: 12, core: 2. Of those that a mesh axis runs over, the one named last changes fastest.
Arguments:
- modal_state: float32 [56, 9, 98304], P(None, None, ('dom', 'sub')), may hold values from -6 to 6
- cluster_id: int32 [98304], P(('dom', 'sub')), may hold values 0 or 1
- jacobian_id: int32 [98304], P(('dom', 'sub')), may hold values from 0 to 63
- face_neighbour: int32 [4, 98304], P(None, ('dom', 'sub')), may hold values from 0 to 320, as said below
- flux_index: int32 [4, 98304], P(None, ('dom', 'sub')), may hold values from 0 to 11, as said below
- send_list: int32 [147456], P(('dom', 'sub')), may hold values from 0 to 511, as said below
- derivative: float32 [3, 56, 56], replicated, may hold values from -1.25 to 1.25
- stiffness: float32 [3, 56, 56], replicated, may hold values from -0.75 to 0.75
- restriction: float32 [4, 21, 56], replicated, may hold values from -0.75 to 0.75
- lifting: float32 [4, 56, 21], replicated, may hold values from -1.25 to 1.25
- orientation: float32 [3, 21, 21], replicated, may hold values from -1.25 to 1.25
- star_matrix: float32 [64, 3, 9, 9], replicated, may hold values from -2 to 2
- flux_minus: float32 [64, 4, 9, 9], replicated, may hold values from -2 to 2
- flux_plus: float32 [64, 4, 9, 9], replicated, may hold values from -2 to 2
Outputs:
- new_state: float32 [56, 9, 98304], P(None, None, ('dom', 'sub'))
The draws below stay inside these ranges and needn't reach their ends.
Inputs may be any that keep to these rules, and one draw needn't show every extreme that they name: `face_neighbour`: each device's 4 * 128 faces are all distinct between interior pairs, live ghost slots and faces without neighbour. Slot blocks are symmetric: a live ghost slot of device p for a face F pairs with the peer's slot (as in the reference program) holding the face that neighbours F, and p's own send_list entry at slot g lists F itself. Along dom the devices at both ends have empty outer blocks; some device fills a dom block of 64 slots and every dom group has two sub-blocks sharing 8 faces. For a face whose neighbour is in a ghost slot, flux_index // 3 equals the face number listed in the sender's send_list slot divided by 128. `send_list`: the first 192 faces of a permutation of each device's 4 * 128 faces; slots past a link's count list faces without a neighbour.
All inputs are finite; a program needn't handle non-finite values. No bound on the sum of `cluster_id` on one device may be relied on, other than what follows from the above.
Results may differ from the reference program's by a relative error of at most 0.0003.
Values sent between devices are 32-bit elements; how exact they have to be, the bound alone decides.
A program may use at most 64 MiB of HBM per device.

```python
import math
import jax
import jax.numpy as jnp
from jax import lax

ORDER = 6
VARS = 9
BASIS = 56
FACE_BASIS = 21
NJ = 64
E_DEV = 128
CAP_DOM = 64
CAP_SUB = 8
ELEMS = 98304
N_DOM = 96
N_SUB = 8


def peer_tables_drawn():
    devices = N_DOM * N_SUB
    ghosts = 2 * CAP_DOM + N_SUB * CAP_SUB
    slot = jnp.arange(ghosts, dtype=jnp.int32)
    in_dom = slot < 2 * CAP_DOM
    upper = jnp.logical_and(slot >= CAP_DOM, in_dom)
    dom_pos = slot % CAP_DOM
    remain = jnp.maximum(slot - 2 * CAP_DOM, 0)
    target = remain // CAP_SUB
    sub_pos = remain % CAP_SUB
    device = jnp.arange(devices, dtype=jnp.int32)
    dom_of = (device // N_SUB)[:, None]
    sub_of = (device % N_SUB)[:, None]
    peer_dom = jnp.where(in_dom[None], dom_of + jnp.where(upper, 1, -1)[None], dom_of)
    peer_dom = jnp.clip(peer_dom, 0, N_DOM - 1)
    peer_sub = jnp.where(in_dom[None], sub_of, target[None])
    peer_slot = jnp.where(in_dom[None], jnp.where(upper, dom_pos, CAP_DOM + dom_pos)[None], 2 * CAP_DOM + sub_of * CAP_SUB + sub_pos[None])
    block = jnp.where(slot < CAP_DOM, 0, jnp.where(in_dom, 1, 2 + target))
    within = jnp.where(in_dom, dom_pos, sub_pos)
    return ((peer_dom * N_SUB + peer_sub).astype(jnp.int32), peer_slot.astype(jnp.int32), block.astype(jnp.int32), within.astype(jnp.int32))


def to_whole(blocked):
    devices = N_DOM * N_SUB
    return jnp.transpose(blocked.reshape(devices, 4, E_DEV), (1, 0, 2)).reshape(4, devices * E_DEV)


def build_mesh(key):
    mesh_key = jax.random.fold_in(key, 17)
    perm_key, dom_key, sub_key, turn_key = jax.random.split(mesh_key, 4)
    devices = N_DOM * N_SUB
    faces = 4 * E_DEV
    ghosts = 2 * CAP_DOM + N_SUB * CAP_SUB
    orders = jax.vmap(lambda single: jax.random.permutation(single, faces))(jax.random.split(perm_key, devices)).astype(jnp.int32)
    dom_links = jax.random.randint(dom_key, (N_DOM - 1, N_SUB), CAP_DOM // 2, CAP_DOM + 1).astype(jnp.int32)
    dom_links = dom_links.at[0, 0].set(CAP_DOM)
    edge_zeros = jnp.zeros((1, N_SUB), jnp.int32)
    padded_links = jnp.concatenate([edge_zeros, dom_links, edge_zeros], axis=0)
    raw_sub = jax.random.randint(sub_key, (N_DOM, N_SUB, N_SUB), 0, CAP_SUB + 1).astype(jnp.int32)
    sub_range = jnp.arange(N_SUB)
    sub_links = jnp.where((sub_range[:, None] < sub_range[None, :])[None], raw_sub, jnp.swapaxes(raw_sub, 1, 2))
    sub_links = jnp.where((sub_range[:, None] == sub_range[None, :])[None], 0, sub_links)
    sub_links = sub_links.at[:, 0, 1].set(CAP_SUB).at[:, 1, 0].set(CAP_SUB)
    device = jnp.arange(devices, dtype=jnp.int32)
    dom_of = device // N_SUB
    sub_of = device % N_SUB
    counts = jnp.concatenate([padded_links[dom_of, sub_of][:, None], padded_links[dom_of + 1, sub_of][:, None], sub_links[dom_of, sub_of]], axis=1)
    peer, peer_slot, block, within = peer_tables_drawn()
    block_counts = jnp.take_along_axis(counts, jnp.broadcast_to(block[None], (devices, ghosts)), axis=1)
    live = within[None, :] < block_counts
    ghost_partner = orders[peer, peer_slot]
    position = jnp.arange(faces, dtype=jnp.int32)
    inner_partner = orders[:, position ^ 1]
    partner = jnp.concatenate([ghost_partner, inner_partner[:, ghosts:]], axis=1)
    live_full = jnp.concatenate([live, jnp.ones((devices, faces - ghosts), bool)], axis=1)
    codes = jnp.where(position[None] < ghosts, jnp.where(live_full, E_DEV + position[None], E_DEV + ghosts), partner % E_DEV)
    turns = jax.random.randint(turn_key, (devices, faces), 0, 3).astype(jnp.int32)
    flux_codes = partner // E_DEV * 3 + turns
    row_ids = jnp.broadcast_to(device[:, None], (devices, faces))
    neighbour = jnp.zeros((devices, faces), jnp.int32).at[row_ids, orders].set(codes.astype(jnp.int32))
    flux_table = jnp.zeros((devices, faces), jnp.int32).at[row_ids, orders].set(flux_codes.astype(jnp.int32))
    return (to_whole(neighbour), to_whole(flux_table), orders[:, :ghosts].reshape(-1))


def draw_face_neighbour(key, part):
    return build_mesh(key)[0]


def draw_flux_index(key, part):
    return build_mesh(key)[1]


def draw_send_list(key, part):
    return build_mesh(key)[2]


def plant(drawn, key, smallest, largest):
    dims = drawn.shape
    place = [jax.random.randint(jax.random.fold_in(key, axis), (), 0, dims[axis]) for axis in range(len(dims))]
    drawn = drawn.at[tuple(place)].set(smallest)
    longest = dims.index(max(dims))
    place[longest] = (place[longest] + 1) % dims[longest]
    return drawn.at[tuple(place)].set(largest)


def block_scale(key, extent, pieces, least, largest):
    def one(dim, blocks):
        steps = jax.random.uniform(jax.random.fold_in(jax.random.fold_in(key, 6), dim), (blocks,), jnp.float32, least / len(pieces), largest / len(pieces))
        return jnp.repeat(jnp.exp(steps), extent[dim] // blocks).reshape((-1,) + (1,) * (len(extent) - dim - 1))

    loudness = one(*pieces[0])
    for cut in pieces[1:]:
        loudness = loudness * one(*cut)
    return loudness


def centred(own_key, extent, width, most, shards=(), held_as=jnp.bfloat16):
    level = block_scale(own_key, extent, shards, -0.22, 0.18) if shards else 1.0
    result = jax.random.normal(own_key, extent, jnp.float32) * width * level
    return jnp.minimum(jnp.maximum(result, -most), most).astype(held_as)


def setup_inputs(seed: int = 0) -> dict:
    arg_keys = jax.random.split(jax.random.key(seed), 15)
    modal_state = centred(arg_keys[0], (BASIS, VARS, ELEMS), 1.0, 6.0, ((2, 768),), jnp.float32)
    cluster_id = plant((jax.random.randint(arg_keys[1], (ELEMS,), 0, 3) < 1).astype(jnp.int32), jax.random.fold_in(arg_keys[1], 1), 0, 1)
    jacobian_id = plant(jax.random.randint(arg_keys[2], (ELEMS,), 0, NJ), jax.random.fold_in(arg_keys[2], 1), 0, NJ - 1).astype(jnp.int32)
    face_neighbour = draw_face_neighbour(jax.random.fold_in(arg_keys[14], 71), 0)
    flux_index = draw_flux_index(jax.random.fold_in(arg_keys[14], 71), 0)
    send_list = draw_send_list(jax.random.fold_in(arg_keys[14], 71), 0)
    derivative = centred(arg_keys[6], (3, BASIS, BASIS), (BASIS * 2 // 5) ** -0.5, 1.25, (), jnp.float32)
    stiffness = centred(arg_keys[7], (3, BASIS, BASIS), BASIS ** -0.5, 0.75, (), jnp.float32)
    restriction = centred(arg_keys[8], (4, FACE_BASIS, BASIS), BASIS ** -0.5, 0.75, (), jnp.float32)
    lifting = centred(arg_keys[9], (4, BASIS, FACE_BASIS), FACE_BASIS ** -0.5, 1.25, (), jnp.float32)
    orientation = centred(arg_keys[10], (3, FACE_BASIS, FACE_BASIS), FACE_BASIS ** -0.5, 1.25, (), jnp.float32)
    star_matrix = centred(arg_keys[11], (NJ, 3, VARS, VARS), VARS ** -0.5, 2.0, (), jnp.float32)
    flux_minus = centred(arg_keys[12], (NJ, 4, VARS, VARS), VARS ** -0.5, 2.0, (), jnp.float32)
    flux_plus = centred(arg_keys[13], (NJ, 4, VARS, VARS), VARS ** -0.5, 2.0, (), jnp.float32)
    return {"modal_state": modal_state, "cluster_id": cluster_id, "jacobian_id": jacobian_id, "face_neighbour": face_neighbour, "flux_index": flux_index, "send_list": send_list, "derivative": derivative, "stiffness": stiffness, "restriction": restriction, "lifting": lifting, "orientation": orientation, "star_matrix": star_matrix, "flux_minus": flux_minus, "flux_plus": flux_plus}


highest = lax.Precision.HIGHEST
step_length = 1.0


def peer_tables():
    devices = N_DOM * N_SUB
    ghosts = 2 * CAP_DOM + N_SUB * CAP_SUB
    slot = jnp.arange(ghosts, dtype=jnp.int32)
    in_dom = slot < 2 * CAP_DOM
    upper = jnp.logical_and(slot >= CAP_DOM, in_dom)
    dom_pos = slot % CAP_DOM
    remain = jnp.maximum(slot - 2 * CAP_DOM, 0)
    target = remain // CAP_SUB
    sub_pos = remain % CAP_SUB
    device = jnp.arange(devices, dtype=jnp.int32)
    dom_of = (device // N_SUB)[:, None]
    sub_of = (device % N_SUB)[:, None]
    peer_dom = jnp.where(in_dom[None], dom_of + jnp.where(upper, 1, -1)[None], dom_of)
    peer_dom = jnp.clip(peer_dom, 0, N_DOM - 1)
    peer_sub = jnp.where(in_dom[None], sub_of, target[None])
    peer_slot = jnp.where(in_dom[None], jnp.where(upper, dom_pos, CAP_DOM + dom_pos)[None], 2 * CAP_DOM + sub_of * CAP_SUB + sub_pos[None])
    return (peer_dom * N_SUB + peer_sub).astype(jnp.int32), peer_slot.astype(jnp.int32)


def lookup(lookup_table, indices):
    onehot = (jnp.arange(lookup_table.shape[0], dtype=jnp.int32)[:, None] == indices[None, :]).astype(lookup_table.dtype)
    return jnp.dot(lookup_table.reshape(lookup_table.shape[0], -1).T, onehot, precision=highest)


def taylor_integrals(values, star_local, derivative, spans):
    taylor_terms = [values]
    current = values
    for degree in range(ORDER - 1):
        following = jnp.zeros_like(values)
        for direction in range(3):
            moved = jnp.einsum('ab,bqe->aqe', derivative[direction], current, precision=highest)
            following = following - jnp.einsum('aqe,qpe->ape', moved, star_local[direction], precision=highest)
        taylor_terms.append(following)
        current = following
    results = []
    for begin_time, end_time in spans:
        summed = jnp.zeros_like(values)
        for degree, taylor_term in enumerate(taylor_terms):
            weight = (end_time ** (degree + 1) - begin_time ** (degree + 1)) / math.factorial(degree + 1)
            summed = summed + weight * taylor_term
        results.append(summed)
    return results


def reference(modal_state, cluster_id, jacobian_id, face_neighbour, flux_index, send_list, derivative, stiffness, restriction, lifting, orientation, star_matrix, flux_minus, flux_plus):
    devices = N_DOM * N_SUB
    elements = E_DEV
    ghosts = 2 * CAP_DOM + N_SUB * CAP_SUB
    basis = modal_state.shape[0]
    variables = modal_state.shape[1]
    peer, peer_slot = peer_tables()
    send_table = send_list.reshape(devices, ghosts)
    ghost_global = peer * elements + send_table[peer, peer_slot] % elements
    codes = face_neighbour.reshape(4, devices, elements)
    dev_index = jnp.broadcast_to(jnp.arange(devices, dtype=jnp.int32)[None, :, None], codes.shape)
    slot = jnp.clip(codes - elements, 0, ghosts - 1)
    global_nbr = jnp.where(codes < elements, dev_index * elements + codes, ghost_global[dev_index, slot])
    valid_face = codes < elements + ghosts
    global_nbr = jnp.where(valid_face, global_nbr, 0).astype(jnp.int32)
    nbr_blocks = jnp.transpose(global_nbr, (1, 0, 2))
    valid_blocks = jnp.transpose(valid_face, (1, 0, 2)).astype(modal_state.dtype)
    flux_blocks = jnp.transpose(flux_index.reshape(4, devices, elements), (1, 0, 2))
    state_blocks = jnp.transpose(modal_state.reshape(basis, variables, devices, elements), (2, 0, 1, 3))
    jac_blocks = jacobian_id.reshape(devices, elements)
    cluster_blocks = cluster_id.reshape(devices, elements)
    half = step_length / 2

    def predict_both(inputs):
        values, jac_part = inputs
        star_local = lookup(star_matrix, jac_part).reshape(3, variables, variables, elements)
        early, later = taylor_integrals(values, star_local, derivative, ((0.0, half), (half, step_length)))
        return early, later

    def predict_half(inputs):
        values, jac_part = inputs
        star_local = lookup(star_matrix, jac_part).reshape(3, variables, variables, elements)
        return taylor_integrals(values, star_local, derivative, ((0.0, half),))[0]

    def make_update(integral_all):
        def update_block(inputs):
            values, jac_part, flux_part, nbr_part, valid_part = inputs
            star_local = lookup(star_matrix, jac_part).reshape(3, variables, variables, elements)
            minus_local = lookup(flux_minus, jac_part).reshape(4, variables, variables, elements)
            plus_local = lookup(flux_plus, jac_part).reshape(4, variables, variables, elements)
            neigh = integral_all[nbr_part // elements, :, :, nbr_part % elements]
            own_face = jnp.einsum('frb,bqe->frqe', restriction, values, precision=highest)
            restrict_sel = restriction[flux_part // 3]
            nbr_face = jnp.einsum('ferb,febq->frqe', restrict_sel, neigh, precision=highest)
            nbr_face = nbr_face * valid_part[:, None, None, :]
            turn_sel = orientation[flux_part % 3]
            oriented = jnp.einsum('ferc,fcqe->frqe', turn_sel, nbr_face, precision=highest)
            combined = jnp.einsum('frqe,fqpe->frpe', own_face, minus_local, precision=highest) + jnp.einsum('frqe,fqpe->frpe', oriented, plus_local, precision=highest)
            lifted = jnp.einsum('fbr,frpe->bpe', lifting, combined, precision=highest)
            weighted = jnp.einsum('cqe,dqpe->dcpe', values, star_local, precision=highest)
            volume = jnp.einsum('dbc,dcpe->bpe', stiffness, weighted, precision=highest)
            return volume + lifted
        return update_block

    first, late = lax.map(predict_both, (state_blocks, jac_blocks))
    middle = state_blocks + lax.map(make_update(first), (first, jac_blocks, flux_blocks, nbr_blocks, valid_blocks))
    fine_half = lax.map(predict_half, (middle, jac_blocks))
    second = jnp.where((cluster_blocks == 1)[:, None, None, :], fine_half, late)
    new_blocks = middle + lax.map(make_update(second), (second, jac_blocks, flux_blocks, nbr_blocks, valid_blocks))
    return jnp.transpose(new_blocks, (1, 2, 0, 3)).reshape(basis, variables, devices * elements)
```

```python
import functools
import math

import jax
import jax.numpy as jnp
from jax import lax
from jax.experimental import pallas as pl
from jax.experimental.pallas import tpu as pltpu
from jax.sharding import PartitionSpec as P

ORDER = 6
CAP_DOM = 64
CAP_SUB = 8
VARS = 9
BASIS = 56
FACE = 21
FPAD = 24
LANES = 128
CLASSES = 64
GHOSTS = 192
PAIRS = VARS * VARS
KDIM = 176
WIDE = 256
F32 = jnp.float32
BF16 = jnp.bfloat16
MESH = pl.DeviceIdType.MESH

half = 0.5
half_weights = [half ** (k + 1) / math.factorial(k + 1) for k in range(ORDER)]
late_weights = [(1.0 - half ** (k + 1)) / math.factorial(k + 1) for k in range(ORDER)]


def split(values):
    high = values.astype(BF16).astype(F32)
    return high, values - high


def left_operand(matrix, pad):
    high, low = split(matrix)
    parts = [high, low, high]
    if pad:
        parts.append(jnp.zeros((matrix.shape[0], pad), F32))
    return jnp.concatenate(parts, axis=1).astype(BF16)


def right_operand(values, pad):
    high, low = split(values)
    parts = [high, high, low]
    if pad:
        parts.append(jnp.zeros((pad, values.shape[1]), F32))
    return jnp.concatenate(parts, axis=0).astype(BF16)


def dot(left, right):
    return jnp.dot(left, right, preferred_element_type=F32)


def lookup(table, onehot):
    high, low = split(table)
    return dot(high.astype(BF16), onehot) + dot(low.astype(BF16), onehot)


def kernel(
    n_dom,
    n_sub,
    state,
    cluster,
    jacobian,
    neighbour,
    flux,
    send,
    derivative,
    stiffness,
    restriction,
    lifting,
    orientation,
    star,
    minus,
    plus,
    out,
    star_rows,
    minus_rows,
    plus_rows,
    left_derivative,
    left_stiffness,
    left_restriction,
    left_lifting,
    left_orientation,
    faces,
    turns,
    pick_send,
    pick_local,
    pick_ghost,
    current,
    moved,
    half_sum,
    late_sum,
    own,
    candidates,
    gathered,
    lift_in,
    payload,
    received,
    send_sem,
    recv_sem,
):
    dom = lax.axis_index("dom")
    sub = lax.axis_index("sub")
    lower = lax.rem(dom + n_dom - 1, n_dom)
    upper = lax.rem(dom + 1, n_dom)
    peers = [(lower, sub), (upper, sub)]
    peers += [(dom, lax.rem(sub + i, n_sub)) for i in range(1, n_sub)]
    barrier = pltpu.get_barrier_semaphore()
    for peer in peers:
        pl.semaphore_signal(barrier, inc=1, device_id=peer, device_id_type=MESH)

    class_id = lax.broadcasted_iota(jnp.int32, (CLASSES, LANES), 0)
    onehot = (class_id == jacobian[...]).astype(F32).astype(BF16)
    for d in range(3):
        star_rows[pl.ds(d * 88, PAIRS), :] = lookup(star[:, d, :], onehot)
    for f in range(4):
        minus_rows[pl.ds(f * 88, PAIRS), :] = lookup(minus[:, f, :], onehot)
        plus_rows[pl.ds(f * 88, PAIRS), :] = lookup(plus[:, f, :], onehot)

    for d in range(3):
        left_derivative[pl.ds(d * BASIS, BASIS), :] = left_operand(-derivative[d], 8)
        left_stiffness[pl.ds(d * BASIS, BASIS), :] = left_operand(stiffness[d], 8)
    faces[...] = jnp.zeros_like(faces)
    for f in range(4):
        faces[pl.ds(f * FPAD, FACE), :] = restriction[:, f, :]
    left_restriction[...] = left_operand(faces[...], 8)
    for f in range(4):
        faces[pl.ds(f * FPAD, FACE), :] = lifting[:, f, :]
    left_lifting[...] = left_operand(jnp.transpose(faces[...]), 0)
    turns[...] = jnp.zeros_like(turns)
    for h in range(3):
        turns[pl.ds(h * FPAD, FACE), pl.ds(0, FACE)] = orientation[h]
    left_orientation[...] = left_operand(turns[...], 0)

    def same(rows, target):
        index = lax.broadcasted_iota(jnp.int32, (rows, LANES), 0)
        return (index == target).astype(F32).astype(BF16)

    for f in range(4):
        code = neighbour[pl.ds(f, 1), :]
        face = flux[pl.ds(f, 1), :] // 3
        inner = jnp.where(code < LANES, face * LANES + code, -1)
        outer = code - LANES
        pick_local[:, pl.ds(f * LANES, LANES)] = same(4 * LANES, inner)
        pick_ghost[:, pl.ds(f * LANES, LANES)] = same(GHOSTS, outer)
    send_column = jnp.transpose(jnp.broadcast_to(send[...], (8, GHOSTS)))[:, :1]
    lane = lax.broadcasted_iota(jnp.int32, (GHOSTS, 4 * LANES), 1)
    pick_send[...] = (lane == send_column).astype(F32).astype(BF16)
    candidates[...] = jnp.zeros_like(candidates)
    out[...] = state[...]

    def mix(left, rows, emit):
        moved[...] = dot(left[...], current[...])
        for first_var in range(0, VARS, 3):
            totals = [None] * 3
            for d in range(3):
                for q in range(VARS):
                    block = moved[pl.ds(d * BASIS, BASIS), pl.ds(q * LANES, LANES)]
                    for i in range(3):
                        row = rows[pl.ds(d * 88 + q * VARS + first_var + i, 1), :]
                        term = block * row
                        totals[i] = term if totals[i] is None else totals[i] + term
            for i in range(3):
                emit(first_var + i, totals[i])

    def put(q, values):
        current[:, pl.ds(q * LANES, LANES)] = right_operand(values, 8)

    def weight(table, degree):
        value = jnp.float32(table[ORDER - 1])
        for k in range(ORDER - 2, 0, -1):
            value = jnp.where(degree == k, jnp.float32(table[k]), value)
        return value

    def phase(step, carry):
        for q in range(VARS):
            values = out[q]
            put(q, values)
            half_sum[q] = values * half_weights[0]
            late_sum[step, q] = values * late_weights[0]

        def degree_step(degree, carry):
            for_half = weight(half_weights, degree)
            for_late = weight(late_weights, degree)

            def emit(p, values):
                half_sum[p] += values * for_half
                late_sum[step, p] += values * for_late
                put(p, values)

            mix(left_derivative, star_rows, emit)
            return carry

        lax.fori_loop(1, ORDER, degree_step, 0)

        use_half = jnp.logical_or(cluster[...] == 1, step == 0)
        for q in range(VARS):
            put(q, jnp.where(use_half, half_sum[q], late_sum[0, q]))

        projected = dot(left_restriction[...], current[...])
        for q in range(VARS):
            for f in range(4):
                tile = projected[f * FPAD : (f + 1) * FPAD, q * LANES : (q + 1) * LANES]
                own[pl.ds(q * FPAD, FPAD), pl.ds(f * LANES, LANES)] = tile
        high, low = split(own[...])
        candidates[pl.ds(0, VARS * FPAD), :] = high.astype(BF16)
        candidates[pl.ds(WIDE, VARS * FPAD), :] = low.astype(BF16)

        both = lax.dot_general(
            pick_send[...], candidates[...], (((1,), (1,)), ((), ())), preferred_element_type=F32
        )
        payload[step] = both[:, :WIDE] + both[:, WIDE:]

        @pl.when(step == 0)
        def _():
            pl.semaphore_wait(barrier, len(peers))

        copies = []
        for i, peer in enumerate(peers):
            if i == 0:
                source, target, count = 0, CAP_DOM, CAP_DOM
            elif i == 1:
                source, target, count = CAP_DOM, 0, CAP_DOM
            else:
                source = pl.multiple_of(2 * CAP_DOM + peer[1] * CAP_SUB, CAP_SUB)
                target = pl.multiple_of(2 * CAP_DOM + sub * CAP_SUB, CAP_SUB)
                count = CAP_SUB
            copy = pltpu.make_async_remote_copy(
                src_ref=payload.at[step, pl.ds(source, count), :],
                dst_ref=received.at[step, pl.ds(target, count), :],
                send_sem=send_sem.at[step, i],
                recv_sem=recv_sem.at[step, i],
                device_id=peer,
                device_id_type=MESH,
            )
            copy.start()
            copies.append(copy)
        mine = pl.multiple_of(2 * CAP_DOM + sub * CAP_SUB, CAP_SUB)
        received[step, pl.ds(mine, CAP_SUB), :] = payload[step, pl.ds(mine, CAP_SUB), :]

        def add_volume(p, values):
            out[p] += values

        mix(left_stiffness, star_rows, add_volume)

        gathered[...] = dot(candidates[pl.ds(0, VARS * FPAD), :], pick_local[...]) + dot(
            candidates[pl.ds(WIDE, VARS * FPAD), :], pick_local[...]
        )
        for copy in copies:
            copy.wait()

        ghosts = jnp.transpose(received[step])[: VARS * FPAD]
        high, low = split(ghosts)
        gathered[...] += dot(high.astype(BF16), pick_ghost[...]) + dot(
            low.astype(BF16), pick_ghost[...]
        )
        turn = lax.rem(flux[...], 3)
        for q in range(VARS):
            turned = dot(
                left_orientation[...], right_operand(gathered[pl.ds(q * FPAD, FPAD), :], 0)
            )
            for f in range(4):
                lanes = slice(f * LANES, (f + 1) * LANES)
                which = turn[f : f + 1]
                gathered[pl.ds(q * FPAD, FPAD), pl.ds(f * LANES, LANES)] = jnp.where(
                    which == 0,
                    turned[:FPAD, lanes],
                    jnp.where(which == 1, turned[FPAD : 2 * FPAD, lanes], turned[2 * FPAD :, lanes]),
                )
        for f in range(4):
            lanes = pl.ds(f * LANES, LANES)
            for first_var in range(0, VARS, 3):
                totals = [None] * 3
                for q in range(VARS):
                    mine_side = own[pl.ds(q * FPAD, FPAD), lanes]
                    other_side = gathered[pl.ds(q * FPAD, FPAD), lanes]
                    for i in range(3):
                        row = f * 88 + q * VARS + first_var + i
                        term = (
                            mine_side * minus_rows[pl.ds(row, 1), :]
                            + other_side * plus_rows[pl.ds(row, 1), :]
                        )
                        totals[i] = term if totals[i] is None else totals[i] + term
                for i in range(3):
                    high, low = split(totals[i])
                    columns = pl.ds((first_var + i) * LANES, LANES)
                    lift_in[0, pl.ds(f * FPAD, FPAD), columns] = high
                    lift_in[1, pl.ds(f * FPAD, FPAD), columns] = low
        high, low = lift_in[0].astype(BF16), lift_in[1].astype(BF16)
        right = jnp.concatenate([high, high, low], axis=0)
        lifted = dot(left_lifting[...], right)
        for p in range(VARS):
            out[p] += lifted[:, p * LANES : (p + 1) * LANES]
        return carry

    lax.fori_loop(0, 2, phase, 0)


def body(
    modal_state,
    cluster_id,
    jacobian_id,
    face_neighbour,
    flux_index,
    send_list,
    derivative,
    stiffness,
    restriction,
    lifting,
    orientation,
    star_matrix,
    flux_minus,
    flux_plus,
):
    n_dom, n_sub = lax.axis_size("dom"), lax.axis_size("sub")
    state = jnp.transpose(modal_state, (1, 0, 2))
    star = jnp.transpose(star_matrix, (2, 3, 1, 0)).reshape(PAIRS, 3, CLASSES)
    minus = jnp.transpose(flux_minus, (2, 3, 1, 0)).reshape(PAIRS, 4, CLASSES)
    plus = jnp.transpose(flux_plus, (2, 3, 1, 0)).reshape(PAIRS, 4, CLASSES)
    vmem = pl.BlockSpec(memory_space=pltpu.VMEM)
    n_peers = n_sub + 1
    result = pl.pallas_call(
        functools.partial(kernel, n_dom, n_sub),
        name="elastic_step",
        out_shape=jax.ShapeDtypeStruct((VARS, BASIS, LANES), F32),
        in_specs=[vmem] * 14,
        out_specs=vmem,
        scratch_shapes=[
            pltpu.VMEM((3 * 88, LANES), F32),
            pltpu.VMEM((4 * 88, LANES), F32),
            pltpu.VMEM((4 * 88, LANES), F32),
            pltpu.VMEM((3 * BASIS, KDIM), BF16),
            pltpu.VMEM((3 * BASIS, KDIM), BF16),
            pltpu.VMEM((4 * FPAD, KDIM), BF16),
            pltpu.VMEM((BASIS, 12 * FPAD), BF16),
            pltpu.VMEM((3 * FPAD, 3 * FPAD), BF16),
            pltpu.VMEM((4 * FPAD, BASIS), F32),
            pltpu.VMEM((3 * FPAD, FPAD), F32),
            pltpu.VMEM((GHOSTS, 4 * LANES), BF16),
            pltpu.VMEM((4 * LANES, 4 * LANES), BF16),
            pltpu.VMEM((GHOSTS, 4 * LANES), BF16),
            pltpu.VMEM((KDIM, VARS * LANES), BF16),
            pltpu.VMEM((3 * BASIS, VARS * LANES), F32),
            pltpu.VMEM((VARS, BASIS, LANES), F32),
            pltpu.VMEM((2, VARS, BASIS, LANES), F32),
            pltpu.VMEM((VARS * FPAD, 4 * LANES), F32),
            pltpu.VMEM((2 * WIDE, 4 * LANES), BF16),
            pltpu.VMEM((VARS * FPAD, 4 * LANES), F32),
            pltpu.VMEM((2, 4 * FPAD, VARS * LANES), F32),
            pltpu.VMEM((2, GHOSTS, WIDE), F32),
            pltpu.VMEM((2, GHOSTS, WIDE), F32),
            pltpu.SemaphoreType.DMA((2, n_peers)),
            pltpu.SemaphoreType.DMA((2, n_peers)),
        ],
        compiler_params=pltpu.CompilerParams(
            collective_id=0, has_side_effects=True, vmem_limit_bytes=48 * 1024 * 1024
        ),
    )(
        state,
        cluster_id.reshape(1, LANES),
        jacobian_id.reshape(1, LANES),
        face_neighbour,
        flux_index,
        send_list.reshape(1, GHOSTS),
        derivative,
        stiffness,
        jnp.transpose(restriction, (1, 0, 2)),
        jnp.transpose(lifting, (2, 0, 1)),
        orientation,
        star,
        minus,
        plus,
    )
    return jnp.transpose(result, (1, 0, 2))


def solution(mesh):
    placed = (
        P(None, None, ("dom", "sub")),
        P(("dom", "sub")),
        P(("dom", "sub")),
        P(None, ("dom", "sub")),
        P(None, ("dom", "sub")),
        P(("dom", "sub")),
        P(),
        P(),
        P(),
        P(),
        P(),
        P(),
        P(),
        P(),
    )
    return jax.shard_map(
        body, mesh=mesh, in_specs=placed, out_specs=P(None, None, ("dom", "sub")), check_vma=False
    )
```

```python
import functools
import math

import jax
import jax.numpy as jnp
from jax import lax
from jax.experimental import pallas as pl
from jax.experimental.pallas import tpu as pltpu
from jax.sharding import PartitionSpec as P

ORDER = 6
CAP_DOM = 64
CAP_SUB = 8
VARS = 9
BASIS = 56
FACE = 21
FPAD = 24
LANES = 128
CLASSES = 64
GHOSTS = 192
PAIRS = VARS * VARS
KDIM = 176
ROWS = VARS * FPAD
WIDE = 256
F32 = jnp.float32
BF16 = jnp.bfloat16
MESH = pl.DeviceIdType.MESH

half = 0.5
half_weights = [half ** (k + 1) / math.factorial(k + 1) for k in range(ORDER)]
late_weights = [(1.0 - half ** (k + 1)) / math.factorial(k + 1) for k in range(ORDER)]


def split(values):
    high = values.astype(BF16).astype(F32)
    return high, values - high


def left_operand(matrix, pad):
    high, low = split(matrix)
    parts = [high, low, high]
    if pad:
        parts.append(jnp.zeros((matrix.shape[0], pad), F32))
    return jnp.concatenate(parts, axis=1).astype(BF16)


def right_operand(values, pad):
    high, low = split(values)
    parts = [high, high, low]
    if pad:
        parts.append(jnp.zeros((pad, values.shape[1]), F32))
    return jnp.concatenate(parts, axis=0).astype(BF16)


def dot(left, right):
    return jnp.dot(left, right, preferred_element_type=F32)


def two_dots(values, right):
    high, low = split(values)
    return dot(high.astype(BF16), right) + dot(low.astype(BF16), right)


def kernel(
    n_dom,
    n_sub,
    remote,
    state_hbm,
    cluster_hbm,
    jacobian_hbm,
    neighbour_hbm,
    flux_hbm,
    send_hbm,
    derivative_hbm,
    stiffness_hbm,
    restriction_hbm,
    lifting_hbm,
    orientation_hbm,
    star_hbm,
    minus_hbm,
    plus_hbm,
    out,
    cluster,
    jacobian,
    neighbour,
    flux,
    send,
    derivative,
    stiffness,
    restriction,
    lifting,
    orientation,
    star,
    minus,
    plus,
    table,
    star_rows,
    minus_rows,
    plus_rows,
    left_derivative,
    left_stiffness,
    left_restriction,
    left_lifting,
    left_orientation,
    faces,
    turns,
    pick_send,
    pick_local,
    pick_ghost,
    current,
    moved,
    half_sum,
    late_sum,
    own,
    other,
    candidates,
    lift_in,
    payload,
    received,
    load_sem,
    send_sem,
    recv_sem,
):
    if remote:
        dom = lax.axis_index("dom")
        sub = lax.axis_index("sub")
        lower = lax.rem(dom + n_dom - 1, n_dom)
        upper = lax.rem(dom + 1, n_dom)
        peers = [(lower, sub), (upper, sub)]
        peers += [(dom, lax.rem(sub + i, n_sub)) for i in range(1, n_sub)]
        barrier = pltpu.get_barrier_semaphore()
        for peer in peers:
            pl.semaphore_signal(barrier, inc=1, device_id=peer, device_id_type=MESH)
    else:
        sub = 0

    loads = {}
    for i, (name, source, target) in enumerate(
        [
            ("jacobian", jacobian_hbm, jacobian),
            ("star", star_hbm, star),
            ("derivative", derivative_hbm, derivative),
            ("state", state_hbm, out),
            ("restriction", restriction_hbm, restriction),
            ("send", send_hbm, send),
            ("cluster", cluster_hbm, cluster),
            ("stiffness", stiffness_hbm, stiffness),
            ("flux", flux_hbm, flux),
            ("neighbour", neighbour_hbm, neighbour),
            ("minus", minus_hbm, minus),
            ("plus", plus_hbm, plus),
            ("orientation", orientation_hbm, orientation),
            ("lifting", lifting_hbm, lifting),
        ]
    ):
        loads[name] = pltpu.make_async_copy(source, target, load_sem.at[i])
        loads[name].start()

    def classes():
        class_id = lax.broadcasted_iota(jnp.int32, (CLASSES, LANES), 0)
        return (class_id == jacobian[...]).astype(F32).astype(BF16)

    loads["jacobian"].wait()
    loads["star"].wait()
    onehot = classes()
    for d in range(3):
        table[pl.ds(0, PAIRS), :] = two_dots(star[:, d, :], onehot)
        for p in range(VARS):
            star_rows[p, pl.ds(d * VARS, VARS), :] = table[pl.ds(p, VARS, stride=VARS), :]
    loads["derivative"].wait()
    for d in range(3):
        left_derivative[pl.ds(d * BASIS, BASIS), :] = left_operand(-derivative[d], 8)
    loads["restriction"].wait()
    faces[...] = jnp.zeros_like(faces)
    for f in range(4):
        faces[pl.ds(f * FPAD, FACE), :] = restriction[:, f, :]
    left_restriction[...] = left_operand(faces[...], 8)
    loads["send"].wait()
    send_column = jnp.transpose(jnp.broadcast_to(send[...], (8, GHOSTS)))[:, :1]
    lane = lax.broadcasted_iota(jnp.int32, (GHOSTS, 4 * LANES), 1)
    pick_send[...] = (lane == send_column).astype(F32).astype(BF16)
    candidates[...] = jnp.zeros_like(candidates)
    loads["cluster"].wait()
    loads["state"].wait()

    def rest_of_setup():
        loads["stiffness"].wait()
        for d in range(3):
            left_stiffness[pl.ds(d * BASIS, BASIS), :] = left_operand(stiffness[d], 8)
        loads["flux"].wait()
        loads["neighbour"].wait()

        def same(rows, target):
            index = lax.broadcasted_iota(jnp.int32, (rows, LANES), 0)
            return (index == target).astype(F32).astype(BF16)

        for f in range(4):
            code = neighbour[pl.ds(f, 1), :]
            face = flux[pl.ds(f, 1), :] // 3
            inner = jnp.where(code < LANES, face * LANES + code, -1)
            outer = code - LANES
            pick_local[:, pl.ds(f * LANES, LANES)] = same(4 * LANES, inner)
            pick_ghost[:, pl.ds(f * LANES, LANES)] = same(GHOSTS, outer)
        loads["minus"].wait()
        loads["plus"].wait()
        onehot = classes()
        for source, rows in ((minus, minus_rows), (plus, plus_rows)):
            table[...] = two_dots(source[...].reshape(4 * PAIRS, CLASSES), onehot)
            for p in range(VARS):
                for f in range(4):
                    rows[p, pl.ds(f * VARS, VARS), :] = table[
                        pl.ds(4 * p + f, VARS, stride=4 * VARS), :
                    ]
        loads["orientation"].wait()
        turns[...] = jnp.zeros_like(turns)
        for h in range(3):
            turns[pl.ds(h * FPAD, FACE), pl.ds(0, FACE)] = orientation[h]
        left_orientation[...] = left_operand(turns[...], 0)
        loads["lifting"].wait()
        for f in range(4):
            faces[pl.ds(f * FPAD, FACE), :] = lifting[:, f, :]
        left_lifting[...] = left_operand(jnp.transpose(faces[...]), 0)

    def mix(left, emit):
        right = jnp.concatenate([current[q] for q in range(VARS)], axis=1)
        result = dot(left[...], right)
        for d in range(3):
            for q in range(VARS):
                moved[d * VARS + q] = result[
                    d * BASIS : (d + 1) * BASIS, q * LANES : (q + 1) * LANES
                ]

        def one_variable(p, carry):
            total = None
            for k in range(3 * VARS):
                term = moved[k] * star_rows[p, pl.ds(k, 1), :]
                total = term if total is None else total + term
            emit(p, total)
            return carry

        lax.fori_loop(0, VARS, one_variable, 0)

    def weight(weights, degree):
        value = jnp.float32(weights[ORDER - 1])
        for k in range(ORDER - 2, 0, -1):
            value = jnp.where(degree == k, jnp.float32(weights[k]), value)
        return value

    def phase(step, carry):
        for q in range(VARS):
            values = out[q]
            current[q] = right_operand(values, 8)
            half_sum[q] = values * half_weights[0]
            late_sum[step, q] = values * late_weights[0]

        def degree_step(degree, carry):
            for_half = weight(half_weights, degree)
            for_late = weight(late_weights, degree)

            def emit(p, values):
                half_sum[p] += values * for_half
                late_sum[step, p] += values * for_late
                current[p] = right_operand(values, 8)

            mix(left_derivative, emit)
            return carry

        lax.fori_loop(1, ORDER, degree_step, 0)

        use_half = jnp.logical_or(cluster[...] == 1, step == 0)
        for q in range(VARS):
            current[q] = right_operand(jnp.where(use_half, half_sum[q], late_sum[0, q]), 8)

        right = jnp.concatenate([current[q] for q in range(VARS)], axis=1)
        projected = dot(left_restriction[...], right)
        for q in range(VARS):
            for f in range(4):
                tile = projected[f * FPAD : (f + 1) * FPAD, q * LANES : (q + 1) * LANES]
                own[f * VARS + q] = tile
                high, low = split(tile)
                lanes = pl.ds(f * LANES, LANES)
                candidates[pl.ds(q * FPAD, FPAD), lanes] = high.astype(BF16)
                candidates[pl.ds(WIDE + q * FPAD, FPAD), lanes] = low.astype(BF16)

        both = lax.dot_general(
            pick_send[...], candidates[...], (((1,), (1,)), ((), ())), preferred_element_type=F32
        )
        payload[step] = both[:, :WIDE] + both[:, WIDE:]
        copies = []
        if remote:

            @pl.when(step == 0)
            def _():
                pl.semaphore_wait(barrier, len(peers))

            for i, peer in enumerate(peers):
                if i == 0:
                    source, target, count = 0, CAP_DOM, CAP_DOM
                elif i == 1:
                    source, target, count = CAP_DOM, 0, CAP_DOM
                else:
                    source = pl.multiple_of(2 * CAP_DOM + peer[1] * CAP_SUB, CAP_SUB)
                    target = pl.multiple_of(2 * CAP_DOM + sub * CAP_SUB, CAP_SUB)
                    count = CAP_SUB
                copy = pltpu.make_async_remote_copy(
                    src_ref=payload.at[step, pl.ds(source, count), :],
                    dst_ref=received.at[step, pl.ds(target, count), :],
                    send_sem=send_sem.at[step, i],
                    recv_sem=recv_sem.at[step, i],
                    device_id=peer,
                    device_id_type=MESH,
                )
                copy.start()
                copies.append(copy)
        mine = pl.multiple_of(2 * CAP_DOM + sub * CAP_SUB, CAP_SUB)
        received[step, pl.ds(mine, CAP_SUB), :] = payload[step, pl.ds(mine, CAP_SUB), :]

        @pl.when(step == 0)
        def _():
            rest_of_setup()

        def add_volume(p, values):
            out[p] += values

        mix(left_stiffness, add_volume)

        turn = lax.rem(flux[...], 3)

        def orient(values):
            for q in range(VARS):
                turned = dot(
                    left_orientation[...], right_operand(values[q * FPAD : (q + 1) * FPAD], 0)
                )
                for f in range(4):
                    lanes = slice(f * LANES, (f + 1) * LANES)
                    which = turn[f : f + 1]
                    other[f * VARS + q] = jnp.where(
                        which == 0,
                        turned[:FPAD, lanes],
                        jnp.where(
                            which == 1,
                            turned[FPAD : 2 * FPAD, lanes],
                            turned[2 * FPAD :, lanes],
                        ),
                    )

        def lift():
            right = jnp.concatenate([lift_in[p] for p in range(VARS)], axis=1)
            lifted = dot(left_lifting[...], right)
            for p in range(VARS):
                out[p] += lifted[:, p * LANES : (p + 1) * LANES]

        orient(
            dot(candidates[pl.ds(0, ROWS), :], pick_local[...])
            + dot(candidates[pl.ds(WIDE, ROWS), :], pick_local[...])
        )

        def both_sides(p, carry):
            tiles = []
            for f in range(4):
                total = None
                for q in range(VARS):
                    k = f * VARS + q
                    term = (
                        own[k] * minus_rows[p, pl.ds(k, 1), :]
                        + other[k] * plus_rows[p, pl.ds(k, 1), :]
                    )
                    total = term if total is None else total + term
                tiles.append(total)
            lift_in[p] = right_operand(jnp.concatenate(tiles, axis=0), 0)
            return carry

        lax.fori_loop(0, VARS, both_sides, 0)
        lift()

        for copy in copies:
            copy.wait()
        ghosts = jnp.transpose(received[step])[:ROWS]
        orient(two_dots(ghosts, pick_ghost[...]))

        def other_side(p, carry):
            tiles = []
            for f in range(4):
                total = None
                for q in range(VARS):
                    k = f * VARS + q
                    term = other[k] * plus_rows[p, pl.ds(k, 1), :]
                    total = term if total is None else total + term
                tiles.append(total)
            lift_in[p] = right_operand(jnp.concatenate(tiles, axis=0), 0)
            return carry

        lax.fori_loop(0, VARS, other_side, 0)
        lift()
        return carry

    lax.fori_loop(0, 2, phase, 0)


def body(
    modal_state,
    cluster_id,
    jacobian_id,
    face_neighbour,
    flux_index,
    send_list,
    derivative,
    stiffness,
    restriction,
    lifting,
    orientation,
    star_matrix,
    flux_minus,
    flux_plus,
    remote=True,
):
    n_dom, n_sub = (lax.axis_size("dom"), lax.axis_size("sub")) if remote else (1, 1)
    operands = (
        jnp.transpose(modal_state, (1, 0, 2)),
        cluster_id.reshape(1, LANES),
        jacobian_id.reshape(1, LANES),
        face_neighbour,
        flux_index,
        send_list.reshape(1, GHOSTS),
        derivative,
        stiffness,
        jnp.transpose(restriction, (1, 0, 2)),
        jnp.transpose(lifting, (2, 0, 1)),
        orientation,
        jnp.transpose(star_matrix, (2, 3, 1, 0)).reshape(PAIRS, 3, CLASSES),
        jnp.transpose(flux_minus, (2, 3, 1, 0)).reshape(PAIRS, 4, CLASSES),
        jnp.transpose(flux_plus, (2, 3, 1, 0)).reshape(PAIRS, 4, CLASSES),
    )
    n_peers = n_sub + 1
    result = pl.pallas_call(
        functools.partial(kernel, n_dom, n_sub, remote),
        name="elastic_step",
        out_shape=jax.ShapeDtypeStruct((VARS, BASIS, LANES), F32),
        in_specs=[pl.BlockSpec(memory_space=pl.ANY)] * len(operands),
        out_specs=pl.BlockSpec(memory_space=pltpu.VMEM),
        scratch_shapes=[pltpu.VMEM(x.shape, x.dtype) for x in operands[1:]]
        + [
            pltpu.VMEM((4 * PAIRS, LANES), F32),
            pltpu.VMEM((VARS, 32, LANES), F32),
            pltpu.VMEM((VARS, 40, LANES), F32),
            pltpu.VMEM((VARS, 40, LANES), F32),
            pltpu.VMEM((3 * BASIS, KDIM), BF16),
            pltpu.VMEM((3 * BASIS, KDIM), BF16),
            pltpu.VMEM((4 * FPAD, KDIM), BF16),
            pltpu.VMEM((BASIS, 12 * FPAD), BF16),
            pltpu.VMEM((3 * FPAD, 3 * FPAD), BF16),
            pltpu.VMEM((4 * FPAD, BASIS), F32),
            pltpu.VMEM((3 * FPAD, FPAD), F32),
            pltpu.VMEM((GHOSTS, 4 * LANES), BF16),
            pltpu.VMEM((4 * LANES, 4 * LANES), BF16),
            pltpu.VMEM((GHOSTS, 4 * LANES), BF16),
            pltpu.VMEM((VARS, KDIM, LANES), BF16),
            pltpu.VMEM((3 * VARS, BASIS, LANES), F32),
            pltpu.VMEM((VARS, BASIS, LANES), F32),
            pltpu.VMEM((2, VARS, BASIS, LANES), F32),
            pltpu.VMEM((4 * VARS, FPAD, LANES), F32),
            pltpu.VMEM((4 * VARS, FPAD, LANES), F32),
            pltpu.VMEM((2 * WIDE, 4 * LANES), BF16),
            pltpu.VMEM((VARS, 12 * FPAD, LANES), BF16),
            pltpu.VMEM((2, GHOSTS, WIDE), F32),
            pltpu.VMEM((2, GHOSTS, WIDE), F32),
            pltpu.SemaphoreType.DMA((len(operands),)),
            pltpu.SemaphoreType.DMA((2, n_peers)),
            pltpu.SemaphoreType.DMA((2, n_peers)),
        ],
        compiler_params=pltpu.CompilerParams(
            collective_id=0 if remote else None,
            has_side_effects=True,
            vmem_limit_bytes=60 * 1024 * 1024,
        ),
    )(*operands)
    return jnp.transpose(result, (1, 0, 2))


def solution(mesh):
    placed = (
        P(None, None, ("dom", "sub")),
        P(("dom", "sub")),
        P(("dom", "sub")),
        P(None, ("dom", "sub")),
        P(None, ("dom", "sub")),
        P(("dom", "sub")),
        P(),
        P(),
        P(),
        P(),
        P(),
        P(),
        P(),
        P(),
    )
    return jax.shard_map(
        body, mesh=mesh, in_specs=placed, out_specs=P(None, None, ("dom", "sub")), check_vma=False
    )
```

```python
import functools
import math

import jax
import jax.numpy as jnp
from jax import lax
from jax.experimental import pallas as pl
from jax.experimental.pallas import tpu as pltpu
from jax.sharding import PartitionSpec as P

ORDER = 6
CAP_DOM = 64
CAP_SUB = 8
VARS = 9
BASIS = 56
FACE = 21
FPAD = 24
LANES = 128
CLASSES = 64
GHOSTS = 192
PAIRS = VARS * VARS
KDIM = 176
ROWS = VARS * FPAD
WIDE = 256
SLOTS = 256
F32 = jnp.float32
BF16 = jnp.bfloat16
MESH = pl.DeviceIdType.MESH

half = 0.5
half_weights = [half ** (k + 1) / math.factorial(k + 1) for k in range(ORDER)]
late_weights = [(1.0 - half ** (k + 1)) / math.factorial(k + 1) for k in range(ORDER)]


def split(values):
    high = values.astype(BF16).astype(F32)
    return high, values - high


def left_operand(matrix, pad):
    high, low = split(matrix)
    parts = [high, low, high]
    if pad:
        parts.append(jnp.zeros((matrix.shape[0], pad), F32))
    return jnp.concatenate(parts, axis=1).astype(BF16)


def right_operand(values, pad):
    high, low = split(values)
    parts = [high, high, low]
    if pad:
        parts.append(jnp.zeros((pad, values.shape[1]), F32))
    return jnp.concatenate(parts, axis=0).astype(BF16)


def dot(left, right):
    return jnp.dot(left, right, preferred_element_type=F32)


def two_dots(values, right):
    high, low = split(values)
    return dot(high.astype(BF16), right) + dot(low.astype(BF16), right)


def kernel(
    n_dom,
    n_sub,
    remote,
    state_hbm,
    cluster_hbm,
    jacobian_hbm,
    neighbour_hbm,
    flux_hbm,
    send_hbm,
    derivative_hbm,
    stiffness_hbm,
    restriction_hbm,
    lifting_hbm,
    orientation_hbm,
    star_hbm,
    minus_hbm,
    plus_hbm,
    out,
    cluster,
    jacobian,
    neighbour,
    flux,
    send,
    derivative,
    stiffness,
    restriction,
    lifting,
    orientation,
    star,
    minus,
    plus,
    table,
    star_rows,
    minus_rows,
    plus_rows,
    left_derivative,
    left_stiffness,
    left_restriction,
    left_lifting,
    left_orientation,
    faces,
    turns,
    pick_send,
    pick_local,
    pick_ghost,
    current,
    moved,
    moved_next,
    half_sum,
    late_sum,
    own,
    other,
    candidates,
    lift_in,
    mixed,
    slot_table,
    slot_rows,
    slot_turn,
    payload,
    received,
    load_sem,
    send_sem,
    recv_sem,
):
    received[:, pl.ds(GHOSTS, SLOTS - GHOSTS), :] = jnp.zeros((2, SLOTS - GHOSTS, WIDE), F32)
    if remote:
        dom = lax.axis_index("dom")
        sub = lax.axis_index("sub")
        lower = lax.rem(dom + n_dom - 1, n_dom)
        upper = lax.rem(dom + 1, n_dom)
        peers = [(lower, sub), (upper, sub)]
        peers += [(dom, lax.rem(sub + i, n_sub)) for i in range(1, n_sub)]
        barrier = pltpu.get_barrier_semaphore()
        for peer in peers:
            pl.semaphore_signal(barrier, inc=1, device_id=peer, device_id_type=MESH)
    else:
        sub = 0

    loads = {}
    for i, (name, source, target) in enumerate(
        [
            ("jacobian", jacobian_hbm, jacobian),
            ("star", star_hbm, star.at[:, pl.ds(0, 3), :]),
            ("derivative", derivative_hbm, derivative),
            ("state", state_hbm, out),
            ("restriction", restriction_hbm, restriction),
            ("send", send_hbm, send),
            ("cluster", cluster_hbm, cluster),
            ("stiffness", stiffness_hbm, stiffness),
            ("flux", flux_hbm, flux),
            ("neighbour", neighbour_hbm, neighbour),
            ("minus", minus_hbm, minus),
            ("plus", plus_hbm, plus),
            ("orientation", orientation_hbm, orientation),
            ("lifting", lifting_hbm, lifting),
        ]
    ):
        loads[name] = pltpu.make_async_copy(source, target, load_sem.at[i])
        loads[name].start()

    def classes():
        class_id = lax.broadcasted_iota(jnp.int32, (CLASSES, LANES), 0)
        return (class_id == jacobian[...]).astype(F32).astype(BF16)

    loads["jacobian"].wait()
    loads["star"].wait()
    onehot = classes()
    table[...] = two_dots(star[...].reshape(4 * PAIRS, CLASSES), onehot)
    for d in range(3):
        for p in range(VARS):
            star_rows[p, pl.ds(d * VARS, VARS), :] = table[
                pl.ds(4 * p + d, VARS, stride=4 * VARS), :
            ]
    loads["derivative"].wait()
    for d in range(3):
        left_derivative[pl.ds(d * BASIS, BASIS), :] = left_operand(-derivative[d], 8)
    loads["restriction"].wait()
    faces[...] = jnp.zeros_like(faces)
    for f in range(4):
        faces[pl.ds(f * FPAD, FACE), :] = restriction[:, f, :]
    left_restriction[...] = left_operand(faces[...], 8)
    loads["send"].wait()
    send_column = jnp.transpose(jnp.broadcast_to(send[...], (8, GHOSTS)))[:, :1]
    lane = lax.broadcasted_iota(jnp.int32, (GHOSTS, 4 * LANES), 1)
    pick_send[pl.ds(0, GHOSTS), :] = (lane == send_column).astype(F32).astype(BF16)
    pick_send[pl.ds(GHOSTS, SLOTS - GHOSTS), :] = jnp.zeros((SLOTS - GHOSTS, 4 * LANES), BF16)
    candidates[...] = jnp.zeros_like(candidates)
    loads["cluster"].wait()
    loads["state"].wait()

    def rest_of_setup():
        loads["stiffness"].wait()
        for d in range(3):
            left_stiffness[pl.ds(d * BASIS, BASIS), :] = left_operand(stiffness[d], 8)
        loads["flux"].wait()
        loads["neighbour"].wait()

        def same(rows, target):
            index = lax.broadcasted_iota(jnp.int32, (rows, LANES), 0)
            return (index == target).astype(F32).astype(BF16)

        for f in range(4):
            code = neighbour[pl.ds(f, 1), :]
            face = flux[pl.ds(f, 1), :] // 3
            inner = jnp.where(code < LANES, face * LANES + code, -1)
            outer = code - LANES
            pick_local[:, pl.ds(f * LANES, LANES)] = same(4 * LANES, inner)
            pick_ghost[:, pl.ds(f * LANES, LANES)] = same(SLOTS, outer)
        loads["minus"].wait()
        loads["plus"].wait()
        onehot = classes()
        for source, rows in ((minus, minus_rows), (plus, plus_rows)):
            table[...] = two_dots(source[...].reshape(4 * PAIRS, CLASSES), onehot)
            for p in range(VARS):
                for f in range(4):
                    rows[p, pl.ds(f * VARS, VARS), :] = table[
                        pl.ds(4 * p + f, VARS, stride=4 * VARS), :
                    ]
            if rows is plus_rows:
                attributes = jnp.concatenate(
                    [
                        jnp.concatenate([jacobian[...]] * 4, axis=1),
                        jnp.concatenate([lax.rem(flux[pl.ds(f, 1), :], 3) for f in range(4)], axis=1),
                        jnp.concatenate([jnp.full((1, LANES), f, jnp.int32) for f in range(4)], axis=1),
                        jnp.zeros((5, 4 * LANES), jnp.int32),
                    ],
                    axis=0,
                )
                slot_data = lax.dot_general(
                    attributes.astype(F32).astype(BF16),
                    pick_send[...],
                    (((1,), (1,)), ((), ())),
                    preferred_element_type=F32,
                ).astype(jnp.int32)
                slot_turn[...] = slot_data[1:2]
                slot_face = slot_data[2:3]
                slot_class = lax.broadcasted_iota(jnp.int32, (CLASSES, SLOTS), 0) == slot_data[:1]
                looked_up = two_dots(
                    source[...].reshape(4 * PAIRS, CLASSES), slot_class.astype(F32).astype(BF16)
                )
                for half_of in range(SLOTS // LANES):
                    slot_table[half_of] = looked_up[:, half_of * LANES : (half_of + 1) * LANES]
                for p in range(VARS):
                    for half_of in range(SLOTS // LANES):
                        lanes = slice(half_of * LANES, (half_of + 1) * LANES)
                        face = slot_face[:, lanes]
                        chosen = None
                        for f in range(4):
                            mine = slot_table[half_of, pl.ds(4 * p + f, VARS, stride=4 * VARS), :]
                            chosen = mine if f == 0 else jnp.where(face == f, mine, chosen)
                        slot_rows[p, pl.ds(0, VARS), lanes] = chosen
        loads["orientation"].wait()
        turns[...] = jnp.zeros_like(turns)
        for h in range(3):
            turns[pl.ds(h * FPAD, FACE), pl.ds(0, FACE)] = orientation[h]
        left_orientation[...] = left_operand(turns[...], 0)
        loads["lifting"].wait()
        for f in range(4):
            faces[pl.ds(f * FPAD, FACE), :] = lifting[:, f, :]
        left_lifting[...] = left_operand(jnp.transpose(faces[...]), 0)

    def project(left, group, target):
        right = current[group[0]]
        if len(group) > 1:
            right = jnp.concatenate([current[q] for q in group], axis=1)
        result = dot(left[...], right)
        for d in range(3):
            for i, q in enumerate(group):
                target[d * VARS + q] = result[
                    d * BASIS : (d + 1) * BASIS, i * LANES : (i + 1) * LANES
                ]

    def mix_several(first_var, count, source):
        totals = [None] * count
        for k in range(3 * VARS):
            block = source[k]
            for i in range(count):
                term = block * star_rows[first_var + i, pl.ds(k, 1), :]
                totals[i] = term if totals[i] is None else totals[i] + term
        return totals

    def mix(left, emit):
        project(left, range(VARS), moved)

        def one_variable(p, carry):
            for i, values in enumerate(mix_several(3 * p, 3, moved)):
                emit(3 * p + i, values)
            return carry

        lax.fori_loop(0, VARS // 3, one_variable, 0)

    def weight(weights, degree):
        value = jnp.float32(weights[ORDER - 1])
        for k in range(ORDER - 2, 0, -1):
            value = jnp.where(degree == k, jnp.float32(weights[k]), value)
        return value

    def phase(step, carry):
        for q in range(VARS):
            values = out[q]
            current[q] = right_operand(values, 8)
            half_sum[q] = values * half_weights[0]
            late_sum[step, q] = values * late_weights[0]

        def degree_step(degree, source, target):
            for_half = weight(half_weights, degree)
            for_late = weight(late_weights, degree)

            def some_variables(first_var, count):
                for i, values in enumerate(mix_several(first_var, count, source)):
                    p = first_var + i
                    half_sum[p] += values * for_half
                    late_sum[step, p] += values * for_late
                    current[p] = right_operand(values, 8)

            for first_var in range(0, VARS, 3):
                some_variables(first_var, 3)
                if target is not None:
                    project(left_derivative, range(first_var, first_var + 3), target)

        project(left_derivative, range(VARS), moved)

        def two_degrees(i, carry):
            degree_step(2 * i + 1, moved, moved_next)
            degree_step(2 * i + 2, moved_next, moved)
            return carry

        lax.fori_loop(0, 2, two_degrees, 0)
        degree_step(5, moved, None)

        use_half = jnp.logical_or(cluster[...] == 1, step == 0)
        for q in range(VARS):
            current[q] = right_operand(jnp.where(use_half, half_sum[q], late_sum[0, q]), 8)

        right = jnp.concatenate([current[q] for q in range(VARS)], axis=1)
        projected = dot(left_restriction[...], right)
        for q in range(VARS):
            for f in range(4):
                tile = projected[f * FPAD : (f + 1) * FPAD, q * LANES : (q + 1) * LANES]
                own[f * VARS + q] = tile
                high, low = split(tile)
                lanes = pl.ds(f * LANES, LANES)
                candidates[pl.ds(q * FPAD, FPAD), lanes] = high.astype(BF16)
                candidates[pl.ds(WIDE + q * FPAD, FPAD), lanes] = low.astype(BF16)

        both = lax.dot_general(
            pick_send[pl.ds(0, GHOSTS), :],
            candidates[...],
            (((1,), (1,)), ((), ())),
            preferred_element_type=F32,
        )
        payload[step] = both[:, :WIDE] + both[:, WIDE:]
        copies = []
        if remote:

            @pl.when(step == 0)
            def _():
                pl.semaphore_wait(barrier, len(peers))

            for i, peer in enumerate(peers):
                if i == 0:
                    source, target, count = 0, CAP_DOM, CAP_DOM
                elif i == 1:
                    source, target, count = CAP_DOM, 0, CAP_DOM
                else:
                    source = pl.multiple_of(2 * CAP_DOM + peer[1] * CAP_SUB, CAP_SUB)
                    target = pl.multiple_of(2 * CAP_DOM + sub * CAP_SUB, CAP_SUB)
                    count = CAP_SUB
                copy = pltpu.make_async_remote_copy(
                    src_ref=payload.at[step, pl.ds(source, count), :],
                    dst_ref=received.at[step, pl.ds(target, count), :],
                    send_sem=send_sem.at[step, i],
                    recv_sem=recv_sem.at[step, i],
                    device_id=peer,
                    device_id_type=MESH,
                )
                copy.start()
                copies.append(copy)
        mine = pl.multiple_of(2 * CAP_DOM + sub * CAP_SUB, CAP_SUB)
        received[step, pl.ds(mine, CAP_SUB), :] = payload[step, pl.ds(mine, CAP_SUB), :]

        @pl.when(step == 0)
        def _():
            rest_of_setup()

        def add_volume(p, values):
            out[p] += values

        mix(left_stiffness, add_volume)

        turn = lax.rem(flux[...], 3)

        def orient(values):
            for q in range(VARS):
                turned = dot(
                    left_orientation[...], right_operand(values[q * FPAD : (q + 1) * FPAD], 0)
                )
                for f in range(4):
                    lanes = slice(f * LANES, (f + 1) * LANES)
                    which = turn[f : f + 1]
                    other[f * VARS + q] = jnp.where(
                        which == 0,
                        turned[:FPAD, lanes],
                        jnp.where(
                            which == 1,
                            turned[FPAD : 2 * FPAD, lanes],
                            turned[2 * FPAD :, lanes],
                        ),
                    )

        def lift():
            right = jnp.concatenate([lift_in[p] for p in range(VARS)], axis=1)
            lifted = dot(left_lifting[...], right)
            for p in range(VARS):
                out[p] += lifted[:, p * LANES : (p + 1) * LANES]

        orient(
            dot(candidates[pl.ds(0, ROWS), :], pick_local[...])
            + dot(candidates[pl.ds(WIDE, ROWS), :], pick_local[...])
        )

        def both_sides(p, carry):
            tiles = []
            for f in range(4):
                total = None
                for q in range(VARS):
                    k = f * VARS + q
                    term = (
                        own[k] * minus_rows[p, pl.ds(k, 1), :]
                        + other[k] * plus_rows[p, pl.ds(k, 1), :]
                    )
                    total = term if total is None else total + term
                tiles.append(total)
            lift_in[p] = right_operand(jnp.concatenate(tiles, axis=0), 0)
            return carry

        lax.fori_loop(0, VARS, both_sides, 0)
        lift()

        for copy in copies:
            copy.wait()
        ghosts = jnp.transpose(received[step])
        turned = dot(
            left_orientation[...],
            jnp.concatenate(
                [right_operand(ghosts[q * FPAD : (q + 1) * FPAD], 0) for q in range(VARS)], axis=1
            ),
        )
        which = slot_turn[...]
        aligned = []
        for q in range(VARS):
            tile = turned[:, q * SLOTS : (q + 1) * SLOTS]
            aligned.append(
                jnp.where(
                    which == 0,
                    tile[:FPAD],
                    jnp.where(which == 1, tile[FPAD : 2 * FPAD], tile[2 * FPAD :]),
                )
            )
        for p in range(VARS):
            total = None
            for q in range(VARS):
                term = aligned[q] * slot_rows[p, pl.ds(q, 1), :]
                total = term if total is None else total + term
            mixed[pl.ds(p * FPAD, FPAD), :] = total
        scattered = two_dots(mixed[...], pick_ghost[...])
        for p in range(VARS):
            tiles = [
                scattered[p * FPAD : (p + 1) * FPAD, f * LANES : (f + 1) * LANES] for f in range(4)
            ]
            lift_in[p] = right_operand(jnp.concatenate(tiles, axis=0), 0)
        lift()
        return carry

    lax.fori_loop(0, 2, phase, 0)


def body(
    modal_state,
    cluster_id,
    jacobian_id,
    face_neighbour,
    flux_index,
    send_list,
    derivative,
    stiffness,
    restriction,
    lifting,
    orientation,
    star_matrix,
    flux_minus,
    flux_plus,
    remote=True,
):
    n_dom, n_sub = (lax.axis_size("dom"), lax.axis_size("sub")) if remote else (1, 1)
    operands = (
        jnp.transpose(modal_state, (1, 0, 2)),
        cluster_id.reshape(1, LANES),
        jacobian_id.reshape(1, LANES),
        face_neighbour,
        flux_index,
        send_list.reshape(1, GHOSTS),
        derivative,
        stiffness,
        jnp.transpose(restriction, (1, 0, 2)),
        jnp.transpose(lifting, (2, 0, 1)),
        orientation,
        jnp.transpose(star_matrix, (2, 3, 1, 0)).reshape(PAIRS, 3, CLASSES),
        jnp.transpose(flux_minus, (2, 3, 1, 0)).reshape(PAIRS, 4, CLASSES),
        jnp.transpose(flux_plus, (2, 3, 1, 0)).reshape(PAIRS, 4, CLASSES),
    )
    operands = tuple(pltpu.with_memory_space_constraint(x, pltpu.HBM) for x in operands)
    n_peers = n_sub + 1
    result = pl.pallas_call(
        functools.partial(kernel, n_dom, n_sub, remote),
        name="elastic_step",
        out_shape=jax.ShapeDtypeStruct((VARS, BASIS, LANES), F32),
        in_specs=[pl.BlockSpec(memory_space=pltpu.HBM)] * len(operands),
        out_specs=pl.BlockSpec(memory_space=pltpu.VMEM),
        scratch_shapes=[
            pltpu.VMEM((PAIRS, 4, CLASSES) if x is operands[11] else x.shape, x.dtype)
            for x in operands[1:]
        ]
        + [
            pltpu.VMEM((4 * PAIRS, LANES), F32),
            pltpu.VMEM((VARS, 32, LANES), F32),
            pltpu.VMEM((VARS, 40, LANES), F32),
            pltpu.VMEM((VARS, 40, LANES), F32),
            pltpu.VMEM((3 * BASIS, KDIM), BF16),
            pltpu.VMEM((3 * BASIS, KDIM), BF16),
            pltpu.VMEM((4 * FPAD, KDIM), BF16),
            pltpu.VMEM((BASIS, 12 * FPAD), BF16),
            pltpu.VMEM((3 * FPAD, 3 * FPAD), BF16),
            pltpu.VMEM((4 * FPAD, BASIS), F32),
            pltpu.VMEM((3 * FPAD, FPAD), F32),
            pltpu.VMEM((SLOTS, 4 * LANES), BF16),
            pltpu.VMEM((4 * LANES, 4 * LANES), BF16),
            pltpu.VMEM((SLOTS, 4 * LANES), BF16),
            pltpu.VMEM((VARS, KDIM, LANES), BF16),
            pltpu.VMEM((3 * VARS, BASIS, LANES), F32),
            pltpu.VMEM((3 * VARS, BASIS, LANES), F32),
            pltpu.VMEM((VARS, BASIS, LANES), F32),
            pltpu.VMEM((2, VARS, BASIS, LANES), F32),
            pltpu.VMEM((4 * VARS, FPAD, LANES), F32),
            pltpu.VMEM((4 * VARS, FPAD, LANES), F32),
            pltpu.VMEM((2 * WIDE, 4 * LANES), BF16),
            pltpu.VMEM((VARS, 12 * FPAD, LANES), BF16),
            pltpu.VMEM((ROWS, SLOTS), F32),
            pltpu.VMEM((2, 4 * PAIRS, LANES), F32),
            pltpu.VMEM((VARS, 16, SLOTS), F32),
            pltpu.VMEM((1, SLOTS), jnp.int32),
            pltpu.VMEM((2, GHOSTS, WIDE), F32),
            pltpu.VMEM((2, SLOTS, WIDE), F32),
            pltpu.SemaphoreType.DMA((len(operands),)),
            pltpu.SemaphoreType.DMA((2, n_peers)),
            pltpu.SemaphoreType.DMA((2, n_peers)),
        ],
        compiler_params=pltpu.CompilerParams(
            collective_id=0 if remote else None,
            has_side_effects=True,
            vmem_limit_bytes=24 * 1024 * 1024,
        ),
    )(*operands)
    return jnp.transpose(result, (1, 0, 2))


def solution(mesh):
    placed = (
        P(None, None, ("dom", "sub")),
        P(("dom", "sub")),
        P(("dom", "sub")),
        P(None, ("dom", "sub")),
        P(None, ("dom", "sub")),
        P(("dom", "sub")),
        P(),
        P(),
        P(),
        P(),
        P(),
        P(),
        P(),
        P(),
    )
    return jax.shard_map(
        body, mesh=mesh, in_specs=placed, out_specs=P(None, None, ("dom", "sub")), check_vma=False
    )
```

```python
import functools
import math

import jax
import jax.numpy as jnp
from jax import lax
from jax.experimental import pallas as pl
from jax.experimental.pallas import tpu as pltpu
from jax.sharding import PartitionSpec as P

ORDER = 6
CAP_DOM = 64
CAP_SUB = 8
VARS = 9
BASIS = 56
FACE = 21
FPAD = 24
LANES = 128
CLASSES = 64
GHOSTS = 192
PAIRS = VARS * VARS
KDIM = 176
ROWS = VARS * FPAD
WIDE = 256
SLOTS = 256
F32 = jnp.float32
BF16 = jnp.bfloat16
MESH = pl.DeviceIdType.MESH

half = 0.5
half_weights = [half ** (k + 1) / math.factorial(k + 1) for k in range(ORDER)]
late_weights = [(1.0 - half ** (k + 1)) / math.factorial(k + 1) for k in range(ORDER)]


def split(values):
    high = values.astype(BF16).astype(F32)
    return high, values - high


def left_operand(matrix, pad):
    high, low = split(matrix)
    parts = [high, low, high]
    if pad:
        parts.append(jnp.zeros((matrix.shape[0], pad), F32))
    return jnp.concatenate(parts, axis=1).astype(BF16)


def right_operand(values, pad):
    high, low = split(values)
    parts = [high, high, low]
    if pad:
        parts.append(jnp.zeros((pad, values.shape[1]), F32))
    return jnp.concatenate(parts, axis=0).astype(BF16)


def dot(left, right):
    return jnp.dot(left, right, preferred_element_type=F32)


def two_dots(values, right):
    high, low = split(values)
    return dot(high.astype(BF16), right) + dot(low.astype(BF16), right)


def kernel(
    n_dom,
    n_sub,
    remote,
    state_hbm,
    cluster_hbm,
    jacobian_hbm,
    neighbour_hbm,
    flux_hbm,
    send_hbm,
    derivative_hbm,
    stiffness_hbm,
    restriction_hbm,
    lifting_hbm,
    orientation_hbm,
    star_hbm,
    minus_hbm,
    plus_hbm,
    out,
    cluster,
    jacobian,
    neighbour,
    flux,
    send,
    derivative,
    stiffness,
    restriction,
    lifting,
    orientation,
    star,
    minus,
    plus,
    table,
    star_rows,
    minus_rows,
    plus_rows,
    left_derivative,
    left_stiffness,
    left_restriction,
    left_lifting,
    left_orientation,
    faces,
    turns,
    pick_send,
    pick_local,
    pick_ghost,
    current,
    moved,
    moved_next,
    half_sum,
    late_sum,
    terms,
    own,
    other,
    candidates,
    lift_in,
    mixed,
    slot_table,
    slot_rows,
    slot_turn,
    payload,
    received,
    load_sem,
    send_sem,
    recv_sem,
):
    received[...] = jnp.zeros_like(received)
    if remote:
        dom = lax.axis_index("dom")
        sub = lax.axis_index("sub")
        has_lower, has_upper = dom > 0, dom < n_dom - 1
        lower = (jnp.maximum(dom - 1, 0), sub)
        upper = (jnp.minimum(dom + 1, n_dom - 1), sub)
        others = [(dom, lax.rem(sub + i, n_sub)) for i in range(1, n_sub)]
        barrier = pltpu.get_barrier_semaphore()

        def greet(peer):
            pl.semaphore_signal(barrier, inc=1, device_id=peer, device_id_type=MESH)

        for peer in others:
            greet(peer)
        pl.when(has_lower)(lambda: greet(lower))
        pl.when(has_upper)(lambda: greet(upper))
    else:
        sub = 0

    loads = {}
    for i, (name, source, target) in enumerate(
        [
            ("jacobian", jacobian_hbm, jacobian),
            ("star", star_hbm, star.at[:, pl.ds(0, 3), :]),
            ("derivative", derivative_hbm, derivative),
            ("state", state_hbm, out),
            ("restriction", restriction_hbm, restriction),
            ("send", send_hbm, send),
            ("cluster", cluster_hbm, cluster),
            ("stiffness", stiffness_hbm, stiffness),
            ("flux", flux_hbm, flux),
            ("neighbour", neighbour_hbm, neighbour),
            ("minus", minus_hbm, minus),
            ("plus", plus_hbm, plus),
            ("orientation", orientation_hbm, orientation),
            ("lifting", lifting_hbm, lifting),
        ]
    ):
        loads[name] = pltpu.make_async_copy(source, target, load_sem.at[i])
        loads[name].start()

    def classes():
        class_id = lax.broadcasted_iota(jnp.int32, (CLASSES, LANES), 0)
        return (class_id == jacobian[...]).astype(F32).astype(BF16)

    loads["jacobian"].wait()
    loads["star"].wait()
    onehot = classes()
    table[...] = two_dots(star[...].reshape(4 * PAIRS, CLASSES), onehot)
    for d in range(3):
        for p in range(VARS):
            star_rows[p, pl.ds(d * VARS, VARS), :] = table[
                pl.ds(4 * p + d, VARS, stride=4 * VARS), :
            ]
    loads["derivative"].wait()
    for d in range(3):
        left_derivative[pl.ds(d * BASIS, BASIS), :] = left_operand(-derivative[d], 8)
    loads["restriction"].wait()
    faces[...] = jnp.zeros_like(faces)
    for f in range(4):
        faces[pl.ds(f * FPAD, FACE), :] = restriction[:, f, :]
    left_restriction[...] = left_operand(faces[...], 8)
    loads["send"].wait()
    send_column = jnp.transpose(jnp.broadcast_to(send[...], (8, GHOSTS)))[:, :1]
    lane = lax.broadcasted_iota(jnp.int32, (GHOSTS, 4 * LANES), 1)
    pick_send[pl.ds(0, GHOSTS), :] = (lane == send_column).astype(F32).astype(BF16)
    pick_send[pl.ds(GHOSTS, SLOTS - GHOSTS), :] = jnp.zeros((SLOTS - GHOSTS, 4 * LANES), BF16)
    candidates[...] = jnp.zeros_like(candidates)
    loads["cluster"].wait()
    loads["state"].wait()

    def rest_of_setup():
        for q in range(VARS):
            total = terms[0, q] * late_weights[0]
            for k in range(1, ORDER):
                total = total + terms[k, q] * late_weights[k]
            late_sum[q] = total
        loads["stiffness"].wait()
        for d in range(3):
            left_stiffness[pl.ds(d * BASIS, BASIS), :] = left_operand(stiffness[d], 8)
        loads["flux"].wait()
        loads["neighbour"].wait()

        def same(rows, target):
            index = lax.broadcasted_iota(jnp.int32, (rows, LANES), 0)
            return (index == target).astype(F32).astype(BF16)

        for f in range(4):
            code = neighbour[pl.ds(f, 1), :]
            face = flux[pl.ds(f, 1), :] // 3
            inner = jnp.where(code < LANES, face * LANES + code, -1)
            outer = code - LANES
            pick_local[:, pl.ds(f * LANES, LANES)] = same(4 * LANES, inner)
            pick_ghost[:, pl.ds(f * LANES, LANES)] = same(SLOTS, outer)
        loads["minus"].wait()
        loads["plus"].wait()
        onehot = classes()
        for source, rows in ((minus, minus_rows), (plus, plus_rows)):
            table[...] = two_dots(source[...].reshape(4 * PAIRS, CLASSES), onehot)
            for p in range(VARS):
                for f in range(4):
                    rows[p, pl.ds(f * VARS, VARS), :] = table[
                        pl.ds(4 * p + f, VARS, stride=4 * VARS), :
                    ]
            if rows is plus_rows:
                attributes = jnp.concatenate(
                    [
                        jnp.concatenate([jacobian[...]] * 4, axis=1),
                        jnp.concatenate([lax.rem(flux[pl.ds(f, 1), :], 3) for f in range(4)], axis=1),
                        jnp.concatenate([jnp.full((1, LANES), f, jnp.int32) for f in range(4)], axis=1),
                        jnp.zeros((5, 4 * LANES), jnp.int32),
                    ],
                    axis=0,
                )
                slot_data = lax.dot_general(
                    attributes.astype(F32).astype(BF16),
                    pick_send[...],
                    (((1,), (1,)), ((), ())),
                    preferred_element_type=F32,
                ).astype(jnp.int32)
                slot_turn[...] = slot_data[1:2]
                slot_face = slot_data[2:3]
                slot_class = lax.broadcasted_iota(jnp.int32, (CLASSES, SLOTS), 0) == slot_data[:1]
                looked_up = two_dots(
                    source[...].reshape(4 * PAIRS, CLASSES), slot_class.astype(F32).astype(BF16)
                )
                for half_of in range(SLOTS // LANES):
                    slot_table[half_of] = looked_up[:, half_of * LANES : (half_of + 1) * LANES]
                for p in range(VARS):
                    for half_of in range(SLOTS // LANES):
                        lanes = slice(half_of * LANES, (half_of + 1) * LANES)
                        face = slot_face[:, lanes]
                        chosen = None
                        for f in range(4):
                            mine = slot_table[half_of, pl.ds(4 * p + f, VARS, stride=4 * VARS), :]
                            chosen = mine if f == 0 else jnp.where(face == f, mine, chosen)
                        slot_rows[p, pl.ds(0, VARS), lanes] = chosen
        loads["orientation"].wait()
        turns[...] = jnp.zeros_like(turns)
        for h in range(3):
            turns[pl.ds(h * FPAD, FACE), pl.ds(0, FACE)] = orientation[h]
        left_orientation[...] = left_operand(turns[...], 0)
        loads["lifting"].wait()
        for f in range(4):
            faces[pl.ds(f * FPAD, FACE), :] = lifting[:, f, :]
        left_lifting[...] = left_operand(jnp.transpose(faces[...]), 0)

    def project(left, group, target):
        right = current[group[0]]
        if len(group) > 1:
            right = jnp.concatenate([current[q] for q in group], axis=1)
        result = dot(left[...], right)
        for d in range(3):
            for i, q in enumerate(group):
                target[d * VARS + q] = result[
                    d * BASIS : (d + 1) * BASIS, i * LANES : (i + 1) * LANES
                ]

    def mix_several(first_var, count, source):
        totals = [None] * count
        for k in range(3 * VARS):
            block = source[k]
            for i in range(count):
                term = block * star_rows[first_var + i, pl.ds(k, 1), :]
                totals[i] = term if totals[i] is None else totals[i] + term
        return totals

    def mix(left, emit):
        project(left, range(VARS), moved)

        def one_variable(p, carry):
            for i, values in enumerate(mix_several(3 * p, 3, moved)):
                emit(3 * p + i, values)
            return carry

        lax.fori_loop(0, VARS // 3, one_variable, 0)

    def weight(weights, degree):
        value = jnp.float32(weights[ORDER - 1])
        for k in range(ORDER - 2, 0, -1):
            value = jnp.where(degree == k, jnp.float32(weights[k]), value)
        return value

    def phase(step, carry):
        for q in range(VARS):
            values = out[q]
            current[q] = right_operand(values, 8)
            half_sum[q] = values * half_weights[0]
            terms[0, q] = values

        def degree_step(degree, source, target):
            for_half = weight(half_weights, degree)

            def some_variables(first_var, count):
                for i, values in enumerate(mix_several(first_var, count, source)):
                    p = first_var + i
                    half_sum[p] += values * for_half
                    terms[degree, p] = values
                    current[p] = right_operand(values, 8)

            for first_var in range(0, VARS, 3):
                some_variables(first_var, 3)
                if target is not None:
                    project(left_derivative, range(first_var, first_var + 3), target)

        project(left_derivative, range(VARS), moved)

        def two_degrees(i, carry):
            degree_step(2 * i + 1, moved, moved_next)
            degree_step(2 * i + 2, moved_next, moved)
            return carry

        lax.fori_loop(0, 2, two_degrees, 0)
        degree_step(5, moved, None)

        use_half = jnp.logical_or(cluster[...] == 1, step == 0)
        for q in range(VARS):
            current[q] = right_operand(jnp.where(use_half, half_sum[q], late_sum[q]), 8)

        right = jnp.concatenate([current[q] for q in range(VARS)], axis=1)
        projected = dot(left_restriction[...], right)
        for q in range(VARS):
            for f in range(4):
                tile = projected[f * FPAD : (f + 1) * FPAD, q * LANES : (q + 1) * LANES]
                own[f * VARS + q] = tile
                high, low = split(tile)
                lanes = pl.ds(f * LANES, LANES)
                candidates[pl.ds(q * FPAD, FPAD), lanes] = high.astype(BF16)
                candidates[pl.ds(WIDE + q * FPAD, FPAD), lanes] = low.astype(BF16)

        both = lax.dot_general(
            pick_send[pl.ds(0, GHOSTS), :],
            candidates[...],
            (((1,), (1,)), ((), ())),
            preferred_element_type=F32,
        )
        payload[step] = both[:, :WIDE] + both[:, WIDE:]
        if remote:

            @pl.when(step == 0)
            def _():
                pl.semaphore_wait(
                    barrier, n_sub - 1 + has_lower.astype(jnp.int32) + has_upper.astype(jnp.int32)
                )

            def transfer(i, peer, source, target, count):
                return pltpu.make_async_remote_copy(
                    src_ref=payload.at[step, pl.ds(source, count), :],
                    dst_ref=received.at[step, pl.ds(target, count), :],
                    send_sem=send_sem.at[step, i],
                    recv_sem=recv_sem.at[step, i],
                    device_id=peer,
                    device_id_type=MESH,
                )

            def to_lower():
                return transfer(0, lower, 0, CAP_DOM, CAP_DOM)

            def to_upper():
                return transfer(1, upper, CAP_DOM, 0, CAP_DOM)

            target = pl.multiple_of(2 * CAP_DOM + sub * CAP_SUB, CAP_SUB)
            copies = []
            for i, peer in enumerate(others):
                source = pl.multiple_of(2 * CAP_DOM + peer[1] * CAP_SUB, CAP_SUB)
                copies.append(transfer(2 + i, peer, source, target, CAP_SUB))
            pl.when(has_lower)(lambda: to_lower().start())
            pl.when(has_upper)(lambda: to_upper().start())
            for copy in copies:
                copy.start()
        mine = pl.multiple_of(2 * CAP_DOM + sub * CAP_SUB, CAP_SUB)
        received[step, pl.ds(mine, CAP_SUB), :] = payload[step, pl.ds(mine, CAP_SUB), :]

        @pl.when(step == 0)
        def _():
            rest_of_setup()

        def add_volume(p, values):
            out[p] += values

        mix(left_stiffness, add_volume)

        turn = lax.rem(flux[...], 3)

        def orient(values):
            for q in range(VARS):
                turned = dot(
                    left_orientation[...], right_operand(values[q * FPAD : (q + 1) * FPAD], 0)
                )
                for f in range(4):
                    lanes = slice(f * LANES, (f + 1) * LANES)
                    which = turn[f : f + 1]
                    other[f * VARS + q] = jnp.where(
                        which == 0,
                        turned[:FPAD, lanes],
                        jnp.where(
                            which == 1,
                            turned[FPAD : 2 * FPAD, lanes],
                            turned[2 * FPAD :, lanes],
                        ),
                    )

        def lift():
            right = jnp.concatenate([lift_in[p] for p in range(VARS)], axis=1)
            lifted = dot(left_lifting[...], right)
            for p in range(VARS):
                out[p] += lifted[:, p * LANES : (p + 1) * LANES]

        orient(
            dot(candidates[pl.ds(0, ROWS), :], pick_local[...])
            + dot(candidates[pl.ds(WIDE, ROWS), :], pick_local[...])
        )

        def both_sides(p, carry):
            tiles = []
            for f in range(4):
                total = None
                for q in range(VARS):
                    k = f * VARS + q
                    term = (
                        own[k] * minus_rows[p, pl.ds(k, 1), :]
                        + other[k] * plus_rows[p, pl.ds(k, 1), :]
                    )
                    total = term if total is None else total + term
                tiles.append(total)
            lift_in[p] = right_operand(jnp.concatenate(tiles, axis=0), 0)
            return carry

        lax.fori_loop(0, VARS, both_sides, 0)
        lift()

        if remote:
            for copy in copies:
                copy.wait()

            @pl.when(has_lower)
            def _():
                to_lower().wait_send()
                to_upper().wait_recv()

            @pl.when(has_upper)
            def _():
                to_upper().wait_send()
                to_lower().wait_recv()

        ghosts = jnp.transpose(received[step])
        turned = dot(
            left_orientation[...],
            jnp.concatenate(
                [right_operand(ghosts[q * FPAD : (q + 1) * FPAD], 0) for q in range(VARS)], axis=1
            ),
        )
        which = slot_turn[...]
        aligned = []
        for q in range(VARS):
            tile = turned[:, q * SLOTS : (q + 1) * SLOTS]
            aligned.append(
                jnp.where(
                    which == 0,
                    tile[:FPAD],
                    jnp.where(which == 1, tile[FPAD : 2 * FPAD], tile[2 * FPAD :]),
                )
            )
        for p in range(VARS):
            total = None
            for q in range(VARS):
                term = aligned[q] * slot_rows[p, pl.ds(q, 1), :]
                total = term if total is None else total + term
            mixed[pl.ds(p * FPAD, FPAD), :] = total
        scattered = two_dots(mixed[...], pick_ghost[...])
        for p in range(VARS):
            tiles = [
                scattered[p * FPAD : (p + 1) * FPAD, f * LANES : (f + 1) * LANES] for f in range(4)
            ]
            lift_in[p] = right_operand(jnp.concatenate(tiles, axis=0), 0)
        lift()
        return carry

    lax.fori_loop(0, 2, phase, 0)


def body(
    modal_state,
    cluster_id,
    jacobian_id,
    face_neighbour,
    flux_index,
    send_list,
    derivative,
    stiffness,
    restriction,
    lifting,
    orientation,
    star_matrix,
    flux_minus,
    flux_plus,
    remote=True,
):
    n_dom, n_sub = (lax.axis_size("dom"), lax.axis_size("sub")) if remote else (1, 1)
    operands = (
        jnp.transpose(modal_state, (1, 0, 2)),
        cluster_id.reshape(1, LANES),
        jacobian_id.reshape(1, LANES),
        face_neighbour,
        flux_index,
        send_list.reshape(1, GHOSTS),
        derivative,
        stiffness,
        jnp.transpose(restriction, (1, 0, 2)),
        jnp.transpose(lifting, (2, 0, 1)),
        orientation,
        jnp.transpose(star_matrix, (2, 3, 1, 0)).reshape(PAIRS, 3, CLASSES),
        jnp.transpose(flux_minus, (2, 3, 1, 0)).reshape(PAIRS, 4, CLASSES),
        jnp.transpose(flux_plus, (2, 3, 1, 0)).reshape(PAIRS, 4, CLASSES),
    )
    operands = tuple(pltpu.with_memory_space_constraint(x, pltpu.HBM) for x in operands)
    n_peers = n_sub + 1
    result = pl.pallas_call(
        functools.partial(kernel, n_dom, n_sub, remote),
        name="elastic_step",
        out_shape=jax.ShapeDtypeStruct((VARS, BASIS, LANES), F32),
        in_specs=[pl.BlockSpec(memory_space=pltpu.HBM)] * len(operands),
        out_specs=pl.BlockSpec(memory_space=pltpu.VMEM),
        scratch_shapes=[
            pltpu.VMEM((PAIRS, 4, CLASSES) if x is operands[11] else x.shape, x.dtype)
            for x in operands[1:]
        ]
        + [
            pltpu.VMEM((4 * PAIRS, LANES), F32),
            pltpu.VMEM((VARS, 32, LANES), F32),
            pltpu.VMEM((VARS, 40, LANES), F32),
            pltpu.VMEM((VARS, 40, LANES), F32),
            pltpu.VMEM((3 * BASIS, KDIM), BF16),
            pltpu.VMEM((3 * BASIS, KDIM), BF16),
            pltpu.VMEM((4 * FPAD, KDIM), BF16),
            pltpu.VMEM((BASIS, 12 * FPAD), BF16),
            pltpu.VMEM((3 * FPAD, 3 * FPAD), BF16),
            pltpu.VMEM((4 * FPAD, BASIS), F32),
            pltpu.VMEM((3 * FPAD, FPAD), F32),
            pltpu.VMEM((SLOTS, 4 * LANES), BF16),
            pltpu.VMEM((4 * LANES, 4 * LANES), BF16),
            pltpu.VMEM((SLOTS, 4 * LANES), BF16),
            pltpu.VMEM((VARS, KDIM, LANES), BF16),
            pltpu.VMEM((3 * VARS, BASIS, LANES), F32),
            pltpu.VMEM((3 * VARS, BASIS, LANES), F32),
            pltpu.VMEM((VARS, BASIS, LANES), F32),
            pltpu.VMEM((VARS, BASIS, LANES), F32),
            pltpu.VMEM((ORDER, VARS, BASIS, LANES), F32),
            pltpu.VMEM((4 * VARS, FPAD, LANES), F32),
            pltpu.VMEM((4 * VARS, FPAD, LANES), F32),
            pltpu.VMEM((2 * WIDE, 4 * LANES), BF16),
            pltpu.VMEM((VARS, 12 * FPAD, LANES), BF16),
            pltpu.VMEM((ROWS, SLOTS), F32),
            pltpu.VMEM((2, 4 * PAIRS, LANES), F32),
            pltpu.VMEM((VARS, 16, SLOTS), F32),
            pltpu.VMEM((1, SLOTS), jnp.int32),
            pltpu.VMEM((2, GHOSTS, WIDE), F32),
            pltpu.VMEM((2, SLOTS, WIDE), F32),
            pltpu.SemaphoreType.DMA((len(operands),)),
            pltpu.SemaphoreType.DMA((2, n_peers)),
            pltpu.SemaphoreType.DMA((2, n_peers)),
        ],
        compiler_params=pltpu.CompilerParams(
            collective_id=0 if remote else None,
            has_side_effects=True,
            vmem_limit_bytes=24 * 1024 * 1024,
        ),
    )(*operands)
    return jnp.transpose(result, (1, 0, 2))


def solution(mesh):
    placed = (
        P(None, None, ("dom", "sub")),
        P(("dom", "sub")),
        P(("dom", "sub")),
        P(None, ("dom", "sub")),
        P(None, ("dom", "sub")),
        P(("dom", "sub")),
        P(),
        P(),
        P(),
        P(),
        P(),
        P(),
        P(),
        P(),
    )
    return jax.shard_map(
        body, mesh=mesh, in_specs=placed, out_specs=P(None, None, ("dom", "sub")), check_vma=False
    )
```

```python
import functools
import math

import jax
import jax.numpy as jnp
from jax import lax
from jax.experimental import pallas as pl
from jax.experimental.pallas import tpu as pltpu
from jax.sharding import PartitionSpec as P

ORDER = 6
CAP_DOM = 64
CAP_SUB = 8
VARS = 9
BASIS = 56
FACE = 21
FPAD = 24
LANES = 128
CLASSES = 64
GHOSTS = 192
PAIRS = VARS * VARS
KDIM = 176
ROWS = VARS * FPAD
WIDE = 256
SLOTS = 256
lead, rest = range(0, 3), range(3, 9)
F32 = jnp.float32
BF16 = jnp.bfloat16
MESH = pl.DeviceIdType.MESH

half = 0.5
half_weights = [half ** (k + 1) / math.factorial(k + 1) for k in range(ORDER)]
late_weights = [(1.0 - half ** (k + 1)) / math.factorial(k + 1) for k in range(ORDER)]


def split(values):
    high = values.astype(BF16).astype(F32)
    return high, values - high


def left_operand(matrix, pad):
    high, low = split(matrix)
    parts = [high, low, high]
    if pad:
        parts.append(jnp.zeros((matrix.shape[0], pad), F32))
    return jnp.concatenate(parts, axis=1).astype(BF16)


def right_operand(values, pad):
    high, low = split(values)
    parts = [high, high, low]
    if pad:
        parts.append(jnp.zeros((pad, values.shape[1]), F32))
    return jnp.concatenate(parts, axis=0).astype(BF16)


def dot(left, right):
    return jnp.dot(left, right, preferred_element_type=F32)


def two_dots(values, right):
    high, low = split(values)
    return dot(high.astype(BF16), right) + dot(low.astype(BF16), right)


def kernel(
    n_dom,
    n_sub,
    remote,
    state_hbm,
    cluster_hbm,
    jacobian_hbm,
    neighbour_hbm,
    flux_hbm,
    send_hbm,
    derivative_hbm,
    stiffness_hbm,
    restriction_hbm,
    lifting_hbm,
    orientation_hbm,
    star_hbm,
    minus_hbm,
    plus_hbm,
    out,
    cluster,
    jacobian,
    neighbour,
    flux,
    send,
    derivative,
    stiffness,
    restriction,
    lifting,
    orientation,
    star,
    minus,
    plus,
    table,
    star_rows,
    minus_rows,
    plus_rows,
    left_derivative,
    left_stiffness,
    left_restriction,
    left_lifting,
    left_orientation,
    faces,
    turns,
    pick_send,
    pick_local,
    pick_ghost,
    current,
    moved,
    partial,
    half_sum,
    late_sum,
    terms,
    own,
    other,
    candidates,
    lift_in,
    mixed,
    slot_table,
    slot_rows,
    slot_turn,
    payload,
    received,
    load_sem,
    send_sem,
    recv_sem,
):
    loads = {}
    for i, (name, source, target) in enumerate(
        [
            ("jacobian", jacobian_hbm, jacobian),
            ("star", star_hbm, star.at[:, pl.ds(0, 3), :]),
            ("derivative", derivative_hbm, derivative),
            ("state", state_hbm, out),
            ("restriction", restriction_hbm, restriction),
            ("send", send_hbm, send),
            ("cluster", cluster_hbm, cluster),
            ("stiffness", stiffness_hbm, stiffness),
            ("flux", flux_hbm, flux),
            ("neighbour", neighbour_hbm, neighbour),
            ("minus", minus_hbm, minus),
            ("plus", plus_hbm, plus),
            ("orientation", orientation_hbm, orientation),
            ("lifting", lifting_hbm, lifting),
        ]
    ):
        loads[name] = pltpu.make_async_copy(source, target, load_sem.at[i])
        loads[name].start()

    received[...] = jnp.zeros_like(received)
    candidates[...] = jnp.zeros_like(candidates)
    faces[...] = jnp.zeros_like(faces)
    if remote:
        dom = lax.axis_index("dom")
        sub = lax.axis_index("sub")
        has_lower, has_upper = dom > 0, dom < n_dom - 1
        lower = (jnp.maximum(dom - 1, 0), sub)
        upper = (jnp.minimum(dom + 1, n_dom - 1), sub)
        others = [(dom, lax.rem(sub + i, n_sub)) for i in range(1, n_sub)]
        barrier = pltpu.get_barrier_semaphore()

        def greet(peer):
            pl.semaphore_signal(barrier, inc=1, device_id=peer, device_id_type=MESH)

        for peer in others:
            greet(peer)
        pl.when(has_lower)(lambda: greet(lower))
        pl.when(has_upper)(lambda: greet(upper))
    else:
        sub = 0

    def classes():
        class_id = lax.broadcasted_iota(jnp.int32, (CLASSES, LANES), 0)
        return (class_id == jacobian[...]).astype(F32).astype(BF16)

    loads["derivative"].wait()
    for d in range(3):
        left_derivative[pl.ds(d * BASIS, BASIS), :] = left_operand(-derivative[d], 8)
    loads["restriction"].wait()
    for f in range(4):
        faces[pl.ds(f * FPAD, FACE), :] = restriction[:, f, :]
    left_restriction[...] = left_operand(faces[...], 8)
    loads["send"].wait()
    send_column = jnp.transpose(jnp.broadcast_to(send[...], (8, GHOSTS)))[:, :1]
    lane = lax.broadcasted_iota(jnp.int32, (GHOSTS, 4 * LANES), 1)
    pick_send[pl.ds(0, GHOSTS), :] = (lane == send_column).astype(F32).astype(BF16)
    pick_send[pl.ds(GHOSTS, SLOTS - GHOSTS), :] = jnp.zeros((SLOTS - GHOSTS, 4 * LANES), BF16)
    loads["jacobian"].wait()
    loads["star"].wait()
    onehot = classes()
    table[...] = two_dots(star[...].reshape(4 * PAIRS, CLASSES), onehot)
    for d in range(3):
        for p in range(VARS):
            star_rows[p, pl.ds(d * VARS, VARS), :] = table[
                pl.ds(4 * p + d, VARS, stride=4 * VARS), :
            ]
    loads["cluster"].wait()
    loads["state"].wait()

    def rest_of_setup():
        for q in range(VARS):
            total = terms[0, q] * late_weights[0]
            for k in range(1, ORDER):
                total = total + terms[k, q] * late_weights[k]
            late_sum[q] = total
        loads["stiffness"].wait()
        for d in range(3):
            left_stiffness[pl.ds(d * BASIS, BASIS), :] = left_operand(stiffness[d], 8)
        loads["flux"].wait()
        loads["neighbour"].wait()

        def same(rows, target):
            index = lax.broadcasted_iota(jnp.int32, (rows, LANES), 0)
            return (index == target).astype(F32).astype(BF16)

        for f in range(4):
            code = neighbour[pl.ds(f, 1), :]
            face = flux[pl.ds(f, 1), :] // 3
            inner = jnp.where(code < LANES, face * LANES + code, -1)
            outer = code - LANES
            pick_local[:, pl.ds(f * LANES, LANES)] = same(4 * LANES, inner)
            pick_ghost[:, pl.ds(f * LANES, LANES)] = same(SLOTS, outer)
        loads["minus"].wait()
        loads["plus"].wait()
        onehot = classes()
        for source, rows in ((minus, minus_rows), (plus, plus_rows)):
            table[...] = two_dots(source[...].reshape(4 * PAIRS, CLASSES), onehot)
            for p in range(VARS):
                for f in range(4):
                    rows[p, pl.ds(f * VARS, VARS), :] = table[
                        pl.ds(4 * p + f, VARS, stride=4 * VARS), :
                    ]
            if rows is plus_rows:
                attributes = jnp.concatenate(
                    [
                        jnp.concatenate([jacobian[...]] * 4, axis=1),
                        jnp.concatenate([lax.rem(flux[pl.ds(f, 1), :], 3) for f in range(4)], axis=1),
                        jnp.concatenate([jnp.full((1, LANES), f, jnp.int32) for f in range(4)], axis=1),
                        jnp.zeros((5, 4 * LANES), jnp.int32),
                    ],
                    axis=0,
                )
                slot_data = lax.dot_general(
                    attributes.astype(F32).astype(BF16),
                    pick_send[...],
                    (((1,), (1,)), ((), ())),
                    preferred_element_type=F32,
                ).astype(jnp.int32)
                slot_turn[...] = slot_data[1:2]
                slot_face = slot_data[2:3]
                slot_class = lax.broadcasted_iota(jnp.int32, (CLASSES, SLOTS), 0) == slot_data[:1]
                looked_up = two_dots(
                    source[...].reshape(4 * PAIRS, CLASSES), slot_class.astype(F32).astype(BF16)
                )
                for half_of in range(SLOTS // LANES):
                    slot_table[half_of] = looked_up[:, half_of * LANES : (half_of + 1) * LANES]
                for p in range(VARS):
                    for half_of in range(SLOTS // LANES):
                        lanes = slice(half_of * LANES, (half_of + 1) * LANES)
                        face = slot_face[:, lanes]
                        chosen = None
                        for f in range(4):
                            mine = slot_table[half_of, pl.ds(4 * p + f, VARS, stride=4 * VARS), :]
                            chosen = mine if f == 0 else jnp.where(face == f, mine, chosen)
                        slot_rows[p, pl.ds(0, VARS), lanes] = chosen
        loads["orientation"].wait()
        turns[...] = jnp.zeros_like(turns)
        for h in range(3):
            turns[pl.ds(h * FPAD, FACE), pl.ds(0, FACE)] = orientation[h]
        left_orientation[...] = left_operand(turns[...], 0)
        loads["lifting"].wait()
        for f in range(4):
            faces[pl.ds(f * FPAD, FACE), :] = lifting[:, f, :]
        left_lifting[...] = left_operand(jnp.transpose(faces[...]), 0)

    def project(left, group, target):
        right = current[group[0]]
        if len(group) > 1:
            right = jnp.concatenate([current[q] for q in group], axis=1)
        result = dot(left[...], right)
        for d in range(3):
            for i, q in enumerate(group):
                target[d * VARS + q] = result[
                    d * BASIS : (d + 1) * BASIS, i * LANES : (i + 1) * LANES
                ]

    def mix_several(first_var, count, source):
        totals = [None] * count
        for k in range(3 * VARS):
            block = source[k]
            for i in range(count):
                term = block * star_rows[first_var + i, pl.ds(k, 1), :]
                totals[i] = term if totals[i] is None else totals[i] + term
        return totals

    def mix(left, emit):
        project(left, range(VARS), moved)

        def one_variable(p, carry):
            for i, values in enumerate(mix_several(3 * p, 3, moved)):
                emit(3 * p + i, values)
            return carry

        lax.fori_loop(0, VARS // 3, one_variable, 0)

    def weight(weights, degree):
        if isinstance(degree, int):
            return weights[degree]
        value = jnp.float32(weights[ORDER - 1])
        for k in range(ORDER - 2, 0, -1):
            value = jnp.where(degree == k, jnp.float32(weights[k]), value)
        return value

    def phase(step, carry):
        for q in range(VARS):
            values = out[q]
            current[q] = right_operand(values, 8)
            half_sum[q] = values * half_weights[0]
            terms[0, q] = values

        def accumulate(chosen, group, begin, degree=None):
            totals = [None] * len(chosen)
            for q in group:
                for d in range(3):
                    block = moved[d * VARS + q]
                    for i, p in enumerate(chosen):
                        term = block * star_rows[p, pl.ds(d * VARS + q, 1), :]
                        totals[i] = term if totals[i] is None else totals[i] + term
            for p, values in zip(chosen, totals):
                if not begin:
                    values = values + partial[p]
                if degree is None:
                    partial[p] = values
                else:
                    half_sum[p] += values * weight(half_weights, degree)
                    terms[degree, p] = values
                    current[p] = right_operand(values, 8)

        def first_part(degree):
            project(left_derivative, rest, moved)
            for chosen in [(0, 1, 2), (3, 4, 5), (6, 7, 8)]:
                accumulate(chosen, lead, True)
            for chosen in [(0, 1, 2)]:
                accumulate(chosen, rest, False, degree)

        def finish(degree):
            for chosen in [(3, 4, 5), (6, 7, 8)]:
                accumulate(chosen, rest, False, degree)

        def turn_over(degree):
            project(left_derivative, lead, moved)
            if degree is not None:
                finish(degree)
            for chosen in []:
                accumulate(chosen, lead, True)

        def block(work):
            def once(i, carry):
                work()
                return carry

            lax.fori_loop(0, jnp.minimum(step + 1, 1), once, 0)

        def one_degree(degree, carry):
            block(lambda: first_part(degree))
            block(lambda: turn_over(degree))
            return carry

        turn_over(None)
        lax.fori_loop(1, ORDER - 1, one_degree, 0)
        block(lambda: first_part(ORDER - 1))
        finish(ORDER - 1)

        use_half = jnp.logical_or(cluster[...] == 1, step == 0)
        for q in range(VARS):
            current[q] = right_operand(jnp.where(use_half, half_sum[q], late_sum[q]), 8)

        right = jnp.concatenate([current[q] for q in range(VARS)], axis=1)
        projected = dot(left_restriction[...], right)
        for q in range(VARS):
            for f in range(4):
                tile = projected[f * FPAD : (f + 1) * FPAD, q * LANES : (q + 1) * LANES]
                own[f * VARS + q] = tile
                high, low = split(tile)
                lanes = pl.ds(f * LANES, LANES)
                candidates[pl.ds(q * FPAD, FPAD), lanes] = high.astype(BF16)
                candidates[pl.ds(WIDE + q * FPAD, FPAD), lanes] = low.astype(BF16)

        both = lax.dot_general(
            pick_send[pl.ds(0, GHOSTS), :],
            candidates[...],
            (((1,), (1,)), ((), ())),
            preferred_element_type=F32,
        )
        payload[step] = both[:, :WIDE] + both[:, WIDE:]
        if remote:

            @pl.when(step == 0)
            def _():
                pl.semaphore_wait(
                    barrier, n_sub - 1 + has_lower.astype(jnp.int32) + has_upper.astype(jnp.int32)
                )

            def transfer(i, peer, source, target, count):
                return pltpu.make_async_remote_copy(
                    src_ref=payload.at[step, pl.ds(source, count), :],
                    dst_ref=received.at[step, pl.ds(target, count), :],
                    send_sem=send_sem.at[step, i],
                    recv_sem=recv_sem.at[step, i],
                    device_id=peer,
                    device_id_type=MESH,
                )

            def to_lower():
                return transfer(0, lower, 0, CAP_DOM, CAP_DOM)

            def to_upper():
                return transfer(1, upper, CAP_DOM, 0, CAP_DOM)

            target = pl.multiple_of(2 * CAP_DOM + sub * CAP_SUB, CAP_SUB)
            copies = []
            for i, peer in enumerate(others):
                source = pl.multiple_of(2 * CAP_DOM + peer[1] * CAP_SUB, CAP_SUB)
                copies.append(transfer(2 + i, peer, source, target, CAP_SUB))
            pl.when(has_lower)(lambda: to_lower().start())
            pl.when(has_upper)(lambda: to_upper().start())
            for copy in copies:
                copy.start()
        mine = pl.multiple_of(2 * CAP_DOM + sub * CAP_SUB, CAP_SUB)
        received[step, pl.ds(mine, CAP_SUB), :] = payload[step, pl.ds(mine, CAP_SUB), :]

        @pl.when(step == 0)
        def _():
            rest_of_setup()

        def add_volume(p, values):
            out[p] += values

        mix(left_stiffness, add_volume)

        turn = lax.rem(flux[...], 3)

        def orient(values):
            for q in range(VARS):
                turned = dot(
                    left_orientation[...], right_operand(values[q * FPAD : (q + 1) * FPAD], 0)
                )
                for f in range(4):
                    lanes = slice(f * LANES, (f + 1) * LANES)
                    which = turn[f : f + 1]
                    other[f * VARS + q] = jnp.where(
                        which == 0,
                        turned[:FPAD, lanes],
                        jnp.where(
                            which == 1,
                            turned[FPAD : 2 * FPAD, lanes],
                            turned[2 * FPAD :, lanes],
                        ),
                    )

        def lift():
            right = jnp.concatenate([lift_in[p] for p in range(VARS)], axis=1)
            lifted = dot(left_lifting[...], right)
            for p in range(VARS):
                out[p] += lifted[:, p * LANES : (p + 1) * LANES]

        orient(
            dot(candidates[pl.ds(0, ROWS), :], pick_local[...])
            + dot(candidates[pl.ds(WIDE, ROWS), :], pick_local[...])
        )

        def both_sides(p, carry):
            tiles = []
            for f in range(4):
                total = None
                for q in range(VARS):
                    k = f * VARS + q
                    term = (
                        own[k] * minus_rows[p, pl.ds(k, 1), :]
                        + other[k] * plus_rows[p, pl.ds(k, 1), :]
                    )
                    total = term if total is None else total + term
                tiles.append(total)
            lift_in[p] = right_operand(jnp.concatenate(tiles, axis=0), 0)
            return carry

        lax.fori_loop(0, VARS, both_sides, 0)
        lift()

        if remote:
            for copy in copies:
                copy.wait()

            @pl.when(has_lower)
            def _():
                to_lower().wait_send()
                to_upper().wait_recv()

            @pl.when(has_upper)
            def _():
                to_upper().wait_send()
                to_lower().wait_recv()

        ghosts = jnp.transpose(received[step])
        turned = dot(
            left_orientation[...],
            jnp.concatenate(
                [right_operand(ghosts[q * FPAD : (q + 1) * FPAD], 0) for q in range(VARS)], axis=1
            ),
        )
        which = slot_turn[...]
        aligned = []
        for q in range(VARS):
            tile = turned[:, q * SLOTS : (q + 1) * SLOTS]
            aligned.append(
                jnp.where(
                    which == 0,
                    tile[:FPAD],
                    jnp.where(which == 1, tile[FPAD : 2 * FPAD], tile[2 * FPAD :]),
                )
            )
        for p in range(VARS):
            total = None
            for q in range(VARS):
                term = aligned[q] * slot_rows[p, pl.ds(q, 1), :]
                total = term if total is None else total + term
            high, low = split(total)
            mixed[pl.ds(p * FPAD, FPAD), pl.ds(0, SLOTS)] = high.astype(BF16)
            mixed[pl.ds(p * FPAD, FPAD), pl.ds(SLOTS, SLOTS)] = low.astype(BF16)
        scattered = dot(mixed[...], jnp.concatenate([pick_ghost[...]] * 2, axis=0))
        for p in range(VARS):
            tiles = [
                scattered[p * FPAD : (p + 1) * FPAD, f * LANES : (f + 1) * LANES] for f in range(4)
            ]
            lift_in[p] = right_operand(jnp.concatenate(tiles, axis=0), 0)
        lift()
        return carry

    lax.fori_loop(0, 2, phase, 0)


def body(
    modal_state,
    cluster_id,
    jacobian_id,
    face_neighbour,
    flux_index,
    send_list,
    derivative,
    stiffness,
    restriction,
    lifting,
    orientation,
    star_matrix,
    flux_minus,
    flux_plus,
    remote=True,
):
    n_dom, n_sub = (lax.axis_size("dom"), lax.axis_size("sub")) if remote else (1, 1)
    operands = (
        jnp.transpose(modal_state, (1, 0, 2)),
        cluster_id.reshape(1, LANES),
        jacobian_id.reshape(1, LANES),
        face_neighbour,
        flux_index,
        send_list.reshape(1, GHOSTS),
        derivative,
        stiffness,
        jnp.transpose(restriction, (1, 0, 2)),
        jnp.transpose(lifting, (2, 0, 1)),
        orientation,
        jnp.transpose(star_matrix, (2, 3, 1, 0)).reshape(PAIRS, 3, CLASSES),
        jnp.transpose(flux_minus, (2, 3, 1, 0)).reshape(PAIRS, 4, CLASSES),
        jnp.transpose(flux_plus, (2, 3, 1, 0)).reshape(PAIRS, 4, CLASSES),
    )
    operands = tuple(pltpu.with_memory_space_constraint(x, pltpu.HBM) for x in operands)
    n_peers = n_sub + 1
    result = pl.pallas_call(
        functools.partial(kernel, n_dom, n_sub, remote),
        name="elastic_step",
        out_shape=jax.ShapeDtypeStruct((VARS, BASIS, LANES), F32),
        in_specs=[pl.BlockSpec(memory_space=pltpu.HBM)] * len(operands),
        out_specs=pl.BlockSpec(memory_space=pltpu.VMEM),
        scratch_shapes=[
            pltpu.VMEM((PAIRS, 4, CLASSES) if x is operands[11] else x.shape, x.dtype)
            for x in operands[1:]
        ]
        + [
            pltpu.VMEM((4 * PAIRS, LANES), F32),
            pltpu.VMEM((VARS, 32, LANES), F32),
            pltpu.VMEM((VARS, 40, LANES), F32),
            pltpu.VMEM((VARS, 40, LANES), F32),
            pltpu.VMEM((3 * BASIS, KDIM), BF16),
            pltpu.VMEM((3 * BASIS, KDIM), BF16),
            pltpu.VMEM((4 * FPAD, KDIM), BF16),
            pltpu.VMEM((BASIS, 12 * FPAD), BF16),
            pltpu.VMEM((3 * FPAD, 3 * FPAD), BF16),
            pltpu.VMEM((4 * FPAD, BASIS), F32),
            pltpu.VMEM((3 * FPAD, FPAD), F32),
            pltpu.VMEM((SLOTS, 4 * LANES), BF16),
            pltpu.VMEM((4 * LANES, 4 * LANES), BF16),
            pltpu.VMEM((SLOTS, 4 * LANES), BF16),
            pltpu.VMEM((VARS, KDIM, LANES), BF16),
            pltpu.VMEM((3 * VARS, BASIS, LANES), F32),
            pltpu.VMEM((VARS, BASIS, LANES), F32),
            pltpu.VMEM((VARS, BASIS, LANES), F32),
            pltpu.VMEM((VARS, BASIS, LANES), F32),
            pltpu.VMEM((ORDER, VARS, BASIS, LANES), F32),
            pltpu.VMEM((4 * VARS, FPAD, LANES), F32),
            pltpu.VMEM((4 * VARS, FPAD, LANES), F32),
            pltpu.VMEM((2 * WIDE, 4 * LANES), BF16),
            pltpu.VMEM((VARS, 12 * FPAD, LANES), BF16),
            pltpu.VMEM((ROWS, 2 * SLOTS), BF16),
            pltpu.VMEM((2, 4 * PAIRS, LANES), F32),
            pltpu.VMEM((VARS, 16, SLOTS), F32),
            pltpu.VMEM((1, SLOTS), jnp.int32),
            pltpu.VMEM((2, GHOSTS, WIDE), F32),
            pltpu.VMEM((2, SLOTS, WIDE), F32),
            pltpu.SemaphoreType.DMA((len(operands),)),
            pltpu.SemaphoreType.DMA((2, n_peers)),
            pltpu.SemaphoreType.DMA((2, n_peers)),
        ],
        compiler_params=pltpu.CompilerParams(
            collective_id=0 if remote else None,
            has_side_effects=True,
            vmem_limit_bytes=24 * 1024 * 1024,
        ),
    )(*operands)
    return jnp.transpose(result, (1, 0, 2))


def solution(mesh):
    placed = (
        P(None, None, ("dom", "sub")),
        P(("dom", "sub")),
        P(("dom", "sub")),
        P(None, ("dom", "sub")),
        P(None, ("dom", "sub")),
        P(("dom", "sub")),
        P(),
        P(),
        P(),
        P(),
        P(),
        P(),
        P(),
        P(),
    )
    return jax.shard_map(
        body, mesh=mesh, in_specs=placed, out_specs=P(None, None, ("dom", "sub")), check_vma=False
    )
```

```python
import functools
import math

import jax
import jax.numpy as jnp
from jax import lax
from jax.experimental import pallas as pl
from jax.experimental.pallas import tpu as pltpu
from jax.sharding import PartitionSpec as P

ORDER = 6
CAP_DOM = 64
CAP_SUB = 8
VARS = 9
BASIS = 56
FACE = 21
FPAD = 24
LANES = 128
CLASSES = 64
GHOSTS = 192
PAIRS = VARS * VARS
KDIM = 176
ROWS = VARS * FPAD
WIDE = 256
SLOTS = 256
lead, rest = range(0, 3), range(3, 9)
F32 = jnp.float32
BF16 = jnp.bfloat16
MESH = pl.DeviceIdType.MESH

half = 0.5
half_weights = [half ** (k + 1) / math.factorial(k + 1) for k in range(ORDER)]
late_weights = [(1.0 - half ** (k + 1)) / math.factorial(k + 1) for k in range(ORDER)]


def split(values):
    high = values.astype(BF16).astype(F32)
    return high, values - high


def left_operand(matrix, pad):
    high, low = split(matrix)
    parts = [high, low, high]
    if pad:
        parts.append(jnp.zeros((matrix.shape[0], pad), F32))
    return jnp.concatenate(parts, axis=1).astype(BF16)


def right_operand(values, pad):
    high, low = split(values)
    parts = [high, high, low]
    if pad:
        parts.append(jnp.zeros((pad, values.shape[1]), F32))
    return jnp.concatenate(parts, axis=0).astype(BF16)


def dot(left, right):
    return jnp.dot(left, right, preferred_element_type=F32)


def two_dots(values, right):
    high, low = split(values)
    return dot(high.astype(BF16), right) + dot(low.astype(BF16), right)


def kernel(
    n_dom,
    n_sub,
    remote,
    state_hbm,
    cluster_hbm,
    jacobian_hbm,
    neighbour_hbm,
    flux_hbm,
    send_hbm,
    derivative_hbm,
    stiffness_hbm,
    restriction_hbm,
    lifting_hbm,
    orientation_hbm,
    star_hbm,
    minus_hbm,
    plus_hbm,
    out,
    cluster,
    jacobian,
    neighbour,
    flux,
    send,
    derivative,
    stiffness,
    restriction,
    lifting,
    orientation,
    star,
    minus,
    plus,
    table,
    star_rows,
    minus_rows,
    plus_rows,
    left_derivative,
    left_stiffness,
    left_restriction,
    left_lifting,
    left_orientation,
    faces,
    turns,
    pick_send,
    pick_local,
    pick_ghost,
    current,
    moved,
    moved_rest,
    partial,
    half_sum,
    late_sum,
    terms,
    own,
    other,
    candidates,
    lift_in,
    mixed,
    slot_table,
    slot_rows,
    slot_turn,
    payload,
    received,
    load_sem,
    send_sem,
    recv_sem,
):
    loads = {}
    for i, (name, source, target) in enumerate(
        [
            ("jacobian", jacobian_hbm, jacobian),
            ("star", star_hbm, star.at[:, pl.ds(0, 3), :]),
            ("derivative", derivative_hbm, derivative),
            ("state", state_hbm, out),
            ("restriction", restriction_hbm, restriction),
            ("send", send_hbm, send),
            ("cluster", cluster_hbm, cluster),
            ("stiffness", stiffness_hbm, stiffness),
            ("flux", flux_hbm, flux),
            ("neighbour", neighbour_hbm, neighbour),
            ("minus", minus_hbm, minus),
            ("plus", plus_hbm, plus),
            ("orientation", orientation_hbm, orientation),
            ("lifting", lifting_hbm, lifting),
        ]
    ):
        loads[name] = pltpu.make_async_copy(source, target, load_sem.at[i])
        loads[name].start()

    received[...] = jnp.zeros_like(received)
    candidates[...] = jnp.zeros_like(candidates)
    faces[...] = jnp.zeros_like(faces)
    if remote:
        dom = lax.axis_index("dom")
        sub = lax.axis_index("sub")
        has_lower, has_upper = dom > 0, dom < n_dom - 1
        lower = (jnp.maximum(dom - 1, 0), sub)
        upper = (jnp.minimum(dom + 1, n_dom - 1), sub)
        others = [(dom, lax.rem(sub + i, n_sub)) for i in range(1, n_sub)]
        barrier = pltpu.get_barrier_semaphore()

        def greet(peer):
            pl.semaphore_signal(barrier, inc=1, device_id=peer, device_id_type=MESH)

        for peer in others:
            greet(peer)
        pl.when(has_lower)(lambda: greet(lower))
        pl.when(has_upper)(lambda: greet(upper))
    else:
        sub = 0

    def classes():
        class_id = lax.broadcasted_iota(jnp.int32, (CLASSES, LANES), 0)
        return (class_id == jacobian[...]).astype(F32).astype(BF16)

    loads["derivative"].wait()
    for d in range(3):
        left_derivative[pl.ds(d * BASIS, BASIS), :] = left_operand(-derivative[d], 8)
    loads["restriction"].wait()
    for f in range(4):
        faces[pl.ds(f * FPAD, FACE), :] = restriction[:, f, :]
    left_restriction[...] = left_operand(faces[...], 8)
    loads["send"].wait()
    send_column = jnp.transpose(jnp.broadcast_to(send[...], (8, GHOSTS)))[:, :1]
    lane = lax.broadcasted_iota(jnp.int32, (GHOSTS, 4 * LANES), 1)
    pick_send[pl.ds(0, GHOSTS), :] = (lane == send_column).astype(F32).astype(BF16)
    pick_send[pl.ds(GHOSTS, SLOTS - GHOSTS), :] = jnp.zeros((SLOTS - GHOSTS, 4 * LANES), BF16)
    loads["jacobian"].wait()
    loads["star"].wait()
    onehot = classes()
    table[...] = two_dots(star[...].reshape(4 * PAIRS, CLASSES), onehot)
    for d in range(3):
        for p in range(VARS):
            star_rows[p, pl.ds(d * VARS, VARS), :] = table[
                pl.ds(4 * p + d, VARS, stride=4 * VARS), :
            ]
    loads["cluster"].wait()
    loads["state"].wait()

    def rest_of_setup():
        for q in range(VARS):
            total = terms[0, q] * late_weights[0]
            for k in range(1, ORDER):
                total = total + terms[k, q] * late_weights[k]
            late_sum[q] = total
        loads["stiffness"].wait()
        for d in range(3):
            left_stiffness[pl.ds(d * BASIS, BASIS), :] = left_operand(stiffness[d], 8)
        loads["flux"].wait()
        loads["neighbour"].wait()

        def same(rows, target):
            index = lax.broadcasted_iota(jnp.int32, (rows, LANES), 0)
            return (index == target).astype(F32).astype(BF16)

        for f in range(4):
            code = neighbour[pl.ds(f, 1), :]
            face = flux[pl.ds(f, 1), :] // 3
            inner = jnp.where(code < LANES, face * LANES + code, -1)
            outer = code - LANES
            pick_local[:, pl.ds(f * LANES, LANES)] = same(4 * LANES, inner)
            pick_ghost[:, pl.ds(f * LANES, LANES)] = same(SLOTS, outer)
        loads["minus"].wait()
        loads["plus"].wait()
        onehot = classes()
        for source, rows in ((minus, minus_rows), (plus, plus_rows)):
            table[...] = two_dots(source[...].reshape(4 * PAIRS, CLASSES), onehot)
            for p in range(VARS):
                for f in range(4):
                    rows[p, pl.ds(f * VARS, VARS), :] = table[
                        pl.ds(4 * p + f, VARS, stride=4 * VARS), :
                    ]
            if rows is plus_rows:
                attributes = jnp.concatenate(
                    [
                        jnp.concatenate([jacobian[...]] * 4, axis=1),
                        jnp.concatenate([lax.rem(flux[pl.ds(f, 1), :], 3) for f in range(4)], axis=1),
                        jnp.concatenate([jnp.full((1, LANES), f, jnp.int32) for f in range(4)], axis=1),
                        jnp.zeros((5, 4 * LANES), jnp.int32),
                    ],
                    axis=0,
                )
                slot_data = lax.dot_general(
                    attributes.astype(F32).astype(BF16),
                    pick_send[...],
                    (((1,), (1,)), ((), ())),
                    preferred_element_type=F32,
                ).astype(jnp.int32)
                slot_turn[...] = slot_data[1:2]
                slot_face = slot_data[2:3]
                slot_class = lax.broadcasted_iota(jnp.int32, (CLASSES, SLOTS), 0) == slot_data[:1]
                looked_up = two_dots(
                    source[...].reshape(4 * PAIRS, CLASSES), slot_class.astype(F32).astype(BF16)
                )
                for half_of in range(SLOTS // LANES):
                    slot_table[half_of] = looked_up[:, half_of * LANES : (half_of + 1) * LANES]
                for p in range(VARS):
                    for half_of in range(SLOTS // LANES):
                        lanes = slice(half_of * LANES, (half_of + 1) * LANES)
                        face = slot_face[:, lanes]
                        chosen = None
                        for f in range(4):
                            mine = slot_table[half_of, pl.ds(4 * p + f, VARS, stride=4 * VARS), :]
                            chosen = mine if f == 0 else jnp.where(face == f, mine, chosen)
                        slot_rows[p, pl.ds(0, VARS), lanes] = chosen
        loads["orientation"].wait()
        turns[...] = jnp.zeros_like(turns)
        for h in range(3):
            turns[pl.ds(h * FPAD, FACE), pl.ds(0, FACE)] = orientation[h]
        left_orientation[...] = left_operand(turns[...], 0)
        loads["lifting"].wait()
        for f in range(4):
            faces[pl.ds(f * FPAD, FACE), :] = lifting[:, f, :]
        left_lifting[...] = left_operand(jnp.transpose(faces[...]), 0)

    def project(left, group, target):
        right = current[group[0]]
        if len(group) > 1:
            right = jnp.concatenate([current[q] for q in group], axis=1)
        result = dot(left[...], right)
        for d in range(3):
            for i, q in enumerate(group):
                target[d * VARS + q] = result[
                    d * BASIS : (d + 1) * BASIS, i * LANES : (i + 1) * LANES
                ]

    def mix_several(first_var, count, source):
        totals = [None] * count
        for k in range(3 * VARS):
            block = source[k]
            for i in range(count):
                term = block * star_rows[first_var + i, pl.ds(k, 1), :]
                totals[i] = term if totals[i] is None else totals[i] + term
        return totals

    def mix(left, emit):
        project(left, range(VARS), moved)

        def one_variable(p, carry):
            for i, values in enumerate(mix_several(3 * p, 3, moved)):
                emit(3 * p + i, values)
            return carry

        lax.fori_loop(0, VARS // 3, one_variable, 0)

    def weight(weights, degree):
        if isinstance(degree, int):
            return weights[degree]
        value = jnp.float32(weights[ORDER - 1])
        for k in range(ORDER - 2, 0, -1):
            value = jnp.where(degree == k, jnp.float32(weights[k]), value)
        return value

    def phase(step, carry):
        for q in range(VARS):
            values = out[q]
            current[q] = right_operand(values, 8)
            half_sum[q] = values * half_weights[0]
            terms[0, q] = values

        def accumulate(chosen, group, begin, degree=None):
            totals = [None] * len(chosen)
            for q in group:
                for d in range(3):
                    block = (moved if q in lead else moved_rest)[d * VARS + q]
                    for i, p in enumerate(chosen):
                        term = block * star_rows[p, pl.ds(d * VARS + q, 1), :]
                        totals[i] = term if totals[i] is None else totals[i] + term
            for p, values in zip(chosen, totals):
                if not begin:
                    values = values + partial[p]
                if degree is None:
                    partial[p] = values
                else:
                    half_sum[p] += values * weight(half_weights, degree)
                    terms[degree, p] = values
                    current[p] = right_operand(values, 8)

        def first_part(degree):
            for chosen in [(0, 1, 2), (3, 4, 5), (6, 7, 8)]:
                accumulate(chosen, lead, True)
            project(left_derivative, rest, moved_rest)
            for chosen in [(0, 1, 2)]:
                accumulate(chosen, rest, False, degree)

        def finish(degree):
            for chosen in [(3, 4, 5), (6, 7, 8)]:
                accumulate(chosen, rest, False, degree)

        def turn_over(degree):
            if degree is not None:
                accumulate((3, 4, 5), rest, False, degree)
            project(left_derivative, lead, moved)
            if degree is not None:
                accumulate((6, 7, 8), rest, False, degree)

        def block(work):
            def once(i, carry):
                work()
                return carry

            lax.fori_loop(0, jnp.minimum(step + 1, 1), once, 0)

        def one_degree(degree, carry):
            block(lambda: first_part(degree))
            block(lambda: turn_over(degree))
            return carry

        turn_over(None)
        lax.fori_loop(1, ORDER - 1, one_degree, 0)
        block(lambda: first_part(ORDER - 1))
        finish(ORDER - 1)

        use_half = jnp.logical_or(cluster[...] == 1, step == 0)
        for q in range(VARS):
            current[q] = right_operand(jnp.where(use_half, half_sum[q], late_sum[q]), 8)

        right = jnp.concatenate([current[q] for q in range(VARS)], axis=1)
        projected = dot(left_restriction[...], right)
        for q in range(VARS):
            for f in range(4):
                tile = projected[f * FPAD : (f + 1) * FPAD, q * LANES : (q + 1) * LANES]
                own[f * VARS + q] = tile
                high, low = split(tile)
                lanes = pl.ds(f * LANES, LANES)
                candidates[pl.ds(q * FPAD, FPAD), lanes] = high.astype(BF16)
                candidates[pl.ds(WIDE + q * FPAD, FPAD), lanes] = low.astype(BF16)

        both = lax.dot_general(
            pick_send[pl.ds(0, GHOSTS), :],
            candidates[...],
            (((1,), (1,)), ((), ())),
            preferred_element_type=F32,
        )
        payload[step] = both[:, :WIDE] + both[:, WIDE:]
        if remote:

            @pl.when(step == 0)
            def _():
                pl.semaphore_wait(
                    barrier, n_sub - 1 + has_lower.astype(jnp.int32) + has_upper.astype(jnp.int32)
                )

            def transfer(i, peer, source, target, count):
                return pltpu.make_async_remote_copy(
                    src_ref=payload.at[step, pl.ds(source, count), :],
                    dst_ref=received.at[step, pl.ds(target, count), :],
                    send_sem=send_sem.at[step, i],
                    recv_sem=recv_sem.at[step, i],
                    device_id=peer,
                    device_id_type=MESH,
                )

            def to_lower():
                return transfer(0, lower, 0, CAP_DOM, CAP_DOM)

            def to_upper():
                return transfer(1, upper, CAP_DOM, 0, CAP_DOM)

            target = pl.multiple_of(2 * CAP_DOM + sub * CAP_SUB, CAP_SUB)
            copies = []
            for i, peer in enumerate(others):
                source = pl.multiple_of(2 * CAP_DOM + peer[1] * CAP_SUB, CAP_SUB)
                copies.append(transfer(2 + i, peer, source, target, CAP_SUB))
            pl.when(has_lower)(lambda: to_lower().start())
            pl.when(has_upper)(lambda: to_upper().start())
            for copy in copies:
                copy.start()
        mine = pl.multiple_of(2 * CAP_DOM + sub * CAP_SUB, CAP_SUB)
        received[step, pl.ds(mine, CAP_SUB), :] = payload[step, pl.ds(mine, CAP_SUB), :]

        @pl.when(step == 0)
        def _():
            rest_of_setup()

        def add_volume(p, values):
            out[p] += values

        mix(left_stiffness, add_volume)

        turn = lax.rem(flux[...], 3)

        def orient(values):
            for q in range(VARS):
                turned = dot(
                    left_orientation[...], right_operand(values[q * FPAD : (q + 1) * FPAD], 0)
                )
                for f in range(4):
                    lanes = slice(f * LANES, (f + 1) * LANES)
                    which = turn[f : f + 1]
                    other[f * VARS + q] = jnp.where(
                        which == 0,
                        turned[:FPAD, lanes],
                        jnp.where(
                            which == 1,
                            turned[FPAD : 2 * FPAD, lanes],
                            turned[2 * FPAD :, lanes],
                        ),
                    )

        def lift():
            right = jnp.concatenate([lift_in[p] for p in range(VARS)], axis=1)
            lifted = dot(left_lifting[...], right)
            for p in range(VARS):
                out[p] += lifted[:, p * LANES : (p + 1) * LANES]

        orient(
            dot(candidates[pl.ds(0, ROWS), :], pick_local[...])
            + dot(candidates[pl.ds(WIDE, ROWS), :], pick_local[...])
        )

        def both_sides(p, carry):
            tiles = []
            for f in range(4):
                total = None
                for q in range(VARS):
                    k = f * VARS + q
                    term = (
                        own[k] * minus_rows[p, pl.ds(k, 1), :]
                        + other[k] * plus_rows[p, pl.ds(k, 1), :]
                    )
                    total = term if total is None else total + term
                tiles.append(total)
            lift_in[p] = right_operand(jnp.concatenate(tiles, axis=0), 0)
            return carry

        lax.fori_loop(0, VARS, both_sides, 0)
        lift()

        if remote:
            for copy in copies:
                copy.wait()

            @pl.when(has_lower)
            def _():
                to_lower().wait_send()
                to_upper().wait_recv()

            @pl.when(has_upper)
            def _():
                to_upper().wait_send()
                to_lower().wait_recv()

        ghosts = jnp.transpose(received[step])
        turned = dot(
            left_orientation[...],
            jnp.concatenate(
                [right_operand(ghosts[q * FPAD : (q + 1) * FPAD], 0) for q in range(VARS)], axis=1
            ),
        )
        which = slot_turn[...]
        aligned = []
        for q in range(VARS):
            tile = turned[:, q * SLOTS : (q + 1) * SLOTS]
            aligned.append(
                jnp.where(
                    which == 0,
                    tile[:FPAD],
                    jnp.where(which == 1, tile[FPAD : 2 * FPAD], tile[2 * FPAD :]),
                )
            )
        for p in range(VARS):
            total = None
            for q in range(VARS):
                term = aligned[q] * slot_rows[p, pl.ds(q, 1), :]
                total = term if total is None else total + term
            high, low = split(total)
            mixed[pl.ds(p * FPAD, FPAD), pl.ds(0, SLOTS)] = high.astype(BF16)
            mixed[pl.ds(p * FPAD, FPAD), pl.ds(SLOTS, SLOTS)] = low.astype(BF16)
        scattered = dot(mixed[...], jnp.concatenate([pick_ghost[...]] * 2, axis=0))
        for p in range(VARS):
            tiles = [
                scattered[p * FPAD : (p + 1) * FPAD, f * LANES : (f + 1) * LANES] for f in range(4)
            ]
            lift_in[p] = right_operand(jnp.concatenate(tiles, axis=0), 0)
        lift()
        return carry

    lax.fori_loop(0, 2, phase, 0)


def body(
    modal_state,
    cluster_id,
    jacobian_id,
    face_neighbour,
    flux_index,
    send_list,
    derivative,
    stiffness,
    restriction,
    lifting,
    orientation,
    star_matrix,
    flux_minus,
    flux_plus,
    remote=True,
):
    n_dom, n_sub = (lax.axis_size("dom"), lax.axis_size("sub")) if remote else (1, 1)
    operands = (
        jnp.transpose(modal_state, (1, 0, 2)),
        cluster_id.reshape(1, LANES),
        jacobian_id.reshape(1, LANES),
        face_neighbour,
        flux_index,
        send_list.reshape(1, GHOSTS),
        derivative,
        stiffness,
        jnp.transpose(restriction, (1, 0, 2)),
        jnp.transpose(lifting, (2, 0, 1)),
        orientation,
        jnp.transpose(star_matrix, (2, 3, 1, 0)).reshape(PAIRS, 3, CLASSES),
        jnp.transpose(flux_minus, (2, 3, 1, 0)).reshape(PAIRS, 4, CLASSES),
        jnp.transpose(flux_plus, (2, 3, 1, 0)).reshape(PAIRS, 4, CLASSES),
    )
    operands = tuple(pltpu.with_memory_space_constraint(x, pltpu.HBM) for x in operands)
    n_peers = n_sub + 1
    result = pl.pallas_call(
        functools.partial(kernel, n_dom, n_sub, remote),
        name="elastic_step",
        out_shape=jax.ShapeDtypeStruct((VARS, BASIS, LANES), F32),
        in_specs=[pl.BlockSpec(memory_space=pltpu.HBM)] * len(operands),
        out_specs=pl.BlockSpec(memory_space=pltpu.VMEM),
        scratch_shapes=[
            pltpu.VMEM((PAIRS, 4, CLASSES) if x is operands[11] else x.shape, x.dtype)
            for x in operands[1:]
        ]
        + [
            pltpu.VMEM((4 * PAIRS, LANES), F32),
            pltpu.VMEM((VARS, 32, LANES), F32),
            pltpu.VMEM((VARS, 40, LANES), F32),
            pltpu.VMEM((VARS, 40, LANES), F32),
            pltpu.VMEM((3 * BASIS, KDIM), BF16),
            pltpu.VMEM((3 * BASIS, KDIM), BF16),
            pltpu.VMEM((4 * FPAD, KDIM), BF16),
            pltpu.VMEM((BASIS, 12 * FPAD), BF16),
            pltpu.VMEM((3 * FPAD, 3 * FPAD), BF16),
            pltpu.VMEM((4 * FPAD, BASIS), F32),
            pltpu.VMEM((3 * FPAD, FPAD), F32),
            pltpu.VMEM((SLOTS, 4 * LANES), BF16),
            pltpu.VMEM((4 * LANES, 4 * LANES), BF16),
            pltpu.VMEM((SLOTS, 4 * LANES), BF16),
            pltpu.VMEM((VARS, KDIM, LANES), BF16),
            pltpu.VMEM((3 * VARS, BASIS, LANES), F32),
            pltpu.VMEM((3 * VARS, BASIS, LANES), F32),
            pltpu.VMEM((VARS, BASIS, LANES), F32),
            pltpu.VMEM((VARS, BASIS, LANES), F32),
            pltpu.VMEM((VARS, BASIS, LANES), F32),
            pltpu.VMEM((ORDER, VARS, BASIS, LANES), F32),
            pltpu.VMEM((4 * VARS, FPAD, LANES), F32),
            pltpu.VMEM((4 * VARS, FPAD, LANES), F32),
            pltpu.VMEM((2 * WIDE, 4 * LANES), BF16),
            pltpu.VMEM((VARS, 12 * FPAD, LANES), BF16),
            pltpu.VMEM((ROWS, 2 * SLOTS), BF16),
            pltpu.VMEM((2, 4 * PAIRS, LANES), F32),
            pltpu.VMEM((VARS, 16, SLOTS), F32),
            pltpu.VMEM((1, SLOTS), jnp.int32),
            pltpu.VMEM((2, GHOSTS, WIDE), F32),
            pltpu.VMEM((2, SLOTS, WIDE), F32),
            pltpu.SemaphoreType.DMA((len(operands),)),
            pltpu.SemaphoreType.DMA((2, n_peers)),
            pltpu.SemaphoreType.DMA((2, n_peers)),
        ],
        compiler_params=pltpu.CompilerParams(
            collective_id=0 if remote else None,
            has_side_effects=True,
            vmem_limit_bytes=24 * 1024 * 1024,
        ),
    )(*operands)
    return jnp.transpose(result, (1, 0, 2))


def solution(mesh):
    placed = (
        P(None, None, ("dom", "sub")),
        P(("dom", "sub")),
        P(("dom", "sub")),
        P(None, ("dom", "sub")),
        P(None, ("dom", "sub")),
        P(("dom", "sub")),
        P(),
        P(),
        P(),
        P(),
        P(),
        P(),
        P(),
        P(),
    )
    return jax.shard_map(
        body, mesh=mesh, in_specs=placed, out_specs=P(None, None, ("dom", "sub")), check_vma=False
    )
```

```python
import functools
import math

import jax
import jax.numpy as jnp
from jax import lax
from jax.experimental import pallas as pl
from jax.experimental.pallas import tpu as pltpu
from jax.sharding import PartitionSpec as P

ORDER = 6
CAP_DOM = 64
CAP_SUB = 8
VARS = 9
BASIS = 56
FACE = 21
FPAD = 24
LANES = 128
CLASSES = 64
GHOSTS = 192
PAIRS = VARS * VARS
KDIM = 176
ROWS = VARS * FPAD
WIDE = 256
SLOTS = 256
lead, rest = range(0, 3), range(3, 9)
F32 = jnp.float32
BF16 = jnp.bfloat16
MESH = pl.DeviceIdType.MESH

half = 0.5
half_weights = [half ** (k + 1) / math.factorial(k + 1) for k in range(ORDER)]
late_weights = [(1.0 - half ** (k + 1)) / math.factorial(k + 1) for k in range(ORDER)]


def split(values):
    high = values.astype(BF16).astype(F32)
    return high, values - high


def left_operand(matrix, pad):
    high, low = split(matrix)
    parts = [high, low, high]
    if pad:
        parts.append(jnp.zeros((matrix.shape[0], pad), F32))
    return jnp.concatenate(parts, axis=1).astype(BF16)


def right_operand(values, pad):
    high, low = split(values)
    parts = [high, high, low]
    if pad:
        parts.append(jnp.zeros((pad, values.shape[1]), F32))
    return jnp.concatenate(parts, axis=0).astype(BF16)


def dot(left, right):
    return jnp.dot(left, right, preferred_element_type=F32)


def two_dots(values, right):
    high, low = split(values)
    return dot(high.astype(BF16), right) + dot(low.astype(BF16), right)


def kernel(
    n_dom,
    n_sub,
    remote,
    state_hbm,
    cluster_hbm,
    jacobian_hbm,
    neighbour_hbm,
    flux_hbm,
    send_hbm,
    derivative_hbm,
    stiffness_hbm,
    restriction_hbm,
    lifting_hbm,
    orientation_hbm,
    star_hbm,
    minus_hbm,
    plus_hbm,
    out,
    cluster,
    jacobian,
    neighbour,
    flux,
    send,
    derivative,
    stiffness,
    restriction,
    lifting,
    orientation,
    star,
    minus,
    plus,
    table,
    star_rows,
    minus_rows,
    plus_rows,
    left_derivative,
    left_stiffness,
    left_restriction,
    left_lifting,
    left_orientation,
    faces,
    turns,
    pick_send,
    pick_local,
    pick_ghost,
    current,
    moved,
    moved_rest,
    partial,
    half_sum,
    late_sum,
    terms,
    own,
    other,
    candidates,
    lift_in,
    mixed,
    slot_table,
    slot_rows,
    slot_turn,
    payload,
    received,
    load_sem,
    send_sem,
    recv_sem,
):
    loads = {}
    for i, (name, source, target) in enumerate(
        [
            ("jacobian", jacobian_hbm, jacobian),
            ("star", star_hbm, star.at[:, pl.ds(0, 3), :]),
            ("derivative", derivative_hbm, derivative),
            ("state", state_hbm, out),
            ("restriction", restriction_hbm, restriction),
            ("send", send_hbm, send),
            ("cluster", cluster_hbm, cluster),
            ("stiffness", stiffness_hbm, stiffness),
            ("flux", flux_hbm, flux),
            ("neighbour", neighbour_hbm, neighbour),
            ("minus", minus_hbm, minus),
            ("plus", plus_hbm, plus),
            ("orientation", orientation_hbm, orientation),
            ("lifting", lifting_hbm, lifting),
        ]
    ):
        loads[name] = pltpu.make_async_copy(source, target, load_sem.at[i])
        loads[name].start()

    received[...] = jnp.zeros_like(received)
    candidates[...] = jnp.zeros_like(candidates)
    faces[...] = jnp.zeros_like(faces)
    if remote:
        dom = lax.axis_index("dom")
        sub = lax.axis_index("sub")
        has_lower, has_upper = dom > 0, dom < n_dom - 1
        lower = (jnp.maximum(dom - 1, 0), sub)
        upper = (jnp.minimum(dom + 1, n_dom - 1), sub)
        others = [(dom, lax.rem(sub + i, n_sub)) for i in range(1, n_sub)]
        barrier = pltpu.get_barrier_semaphore()

        def greet(peer):
            pl.semaphore_signal(barrier, inc=1, device_id=peer, device_id_type=MESH)

        for peer in others:
            greet(peer)
        pl.when(has_lower)(lambda: greet(lower))
        pl.when(has_upper)(lambda: greet(upper))
    else:
        sub = 0

    def classes():
        class_id = lax.broadcasted_iota(jnp.int32, (CLASSES, LANES), 0)
        return (class_id == jacobian[...]).astype(F32).astype(BF16)

    loads["derivative"].wait()
    for d in range(3):
        left_derivative[pl.ds(d * BASIS, BASIS), :] = left_operand(-derivative[d], 8)
    loads["restriction"].wait()
    for f in range(4):
        faces[pl.ds(f * FPAD, FACE), :] = restriction[:, f, :]
    left_restriction[...] = left_operand(faces[...], 8)
    loads["send"].wait()
    send_column = jnp.transpose(jnp.broadcast_to(send[...], (8, GHOSTS)))[:, :1]
    lane = lax.broadcasted_iota(jnp.int32, (GHOSTS, 4 * LANES), 1)
    pick_send[pl.ds(0, GHOSTS), :] = (lane == send_column).astype(F32).astype(BF16)
    pick_send[pl.ds(GHOSTS, SLOTS - GHOSTS), :] = jnp.zeros((SLOTS - GHOSTS, 4 * LANES), BF16)
    loads["jacobian"].wait()
    loads["star"].wait()
    onehot = classes()
    table[...] = two_dots(star[...].reshape(4 * PAIRS, CLASSES), onehot)
    for d in range(3):
        for p in range(VARS):
            star_rows[p, pl.ds(d * VARS, VARS), :] = table[
                pl.ds(4 * p + d, VARS, stride=4 * VARS), :
            ]
    loads["cluster"].wait()
    loads["state"].wait()

    def rest_of_setup():
        for q in range(VARS):
            total = terms[0, q] * late_weights[0]
            for k in range(1, ORDER):
                total = total + terms[k, q] * late_weights[k]
            late_sum[q] = total
        loads["stiffness"].wait()
        for d in range(3):
            left_stiffness[pl.ds(d * BASIS, BASIS), :] = left_operand(stiffness[d], 8)
        loads["flux"].wait()
        loads["neighbour"].wait()

        def same(rows, target):
            index = lax.broadcasted_iota(jnp.int32, (rows, LANES), 0)
            return (index == target).astype(F32).astype(BF16)

        for f in range(4):
            code = neighbour[pl.ds(f, 1), :]
            face = flux[pl.ds(f, 1), :] // 3
            inner = jnp.where(code < LANES, face * LANES + code, -1)
            outer = code - LANES
            pick_local[:, pl.ds(f * LANES, LANES)] = same(4 * LANES, inner)
            pick_ghost[:, pl.ds(f * LANES, LANES)] = same(SLOTS, outer)
        loads["minus"].wait()
        loads["plus"].wait()
        onehot = classes()
        for source, rows in ((minus, minus_rows), (plus, plus_rows)):
            table[...] = two_dots(source[...].reshape(4 * PAIRS, CLASSES), onehot)
            for p in range(VARS):
                for f in range(4):
                    rows[p, pl.ds(f * VARS, VARS), :] = table[
                        pl.ds(4 * p + f, VARS, stride=4 * VARS), :
                    ]
            if rows is plus_rows:
                attributes = jnp.concatenate(
                    [
                        jnp.concatenate([jacobian[...]] * 4, axis=1),
                        jnp.concatenate([lax.rem(flux[pl.ds(f, 1), :], 3) for f in range(4)], axis=1),
                        jnp.concatenate([jnp.full((1, LANES), f, jnp.int32) for f in range(4)], axis=1),
                        jnp.zeros((5, 4 * LANES), jnp.int32),
                    ],
                    axis=0,
                )
                slot_data = lax.dot_general(
                    attributes.astype(F32).astype(BF16),
                    pick_send[...],
                    (((1,), (1,)), ((), ())),
                    preferred_element_type=F32,
                ).astype(jnp.int32)
                slot_turn[...] = slot_data[1:2]
                slot_face = slot_data[2:3]
                slot_class = lax.broadcasted_iota(jnp.int32, (CLASSES, SLOTS), 0) == slot_data[:1]
                looked_up = two_dots(
                    source[...].reshape(4 * PAIRS, CLASSES), slot_class.astype(F32).astype(BF16)
                )
                for half_of in range(SLOTS // LANES):
                    slot_table[half_of] = looked_up[:, half_of * LANES : (half_of + 1) * LANES]
                for p in range(VARS):
                    for half_of in range(SLOTS // LANES):
                        lanes = slice(half_of * LANES, (half_of + 1) * LANES)
                        face = slot_face[:, lanes]
                        chosen = None
                        for f in range(4):
                            mine = slot_table[half_of, pl.ds(4 * p + f, VARS, stride=4 * VARS), :]
                            chosen = mine if f == 0 else jnp.where(face == f, mine, chosen)
                        slot_rows[p, pl.ds(0, VARS), lanes] = chosen
        loads["orientation"].wait()
        turns[...] = jnp.zeros_like(turns)
        for h in range(3):
            turns[pl.ds(h * FPAD, FACE), pl.ds(0, FACE)] = orientation[h]
        left_orientation[...] = left_operand(turns[...], 0)
        loads["lifting"].wait()
        for f in range(4):
            faces[pl.ds(f * FPAD, FACE), :] = lifting[:, f, :]
        left_lifting[...] = left_operand(jnp.transpose(faces[...]), 0)

    def project(left, group, target):
        right = current[group[0]]
        if len(group) > 1:
            right = jnp.concatenate([current[q] for q in group], axis=1)
        result = dot(left[...], right)
        for d in range(3):
            for i, q in enumerate(group):
                target[d * VARS + q] = result[
                    d * BASIS : (d + 1) * BASIS, i * LANES : (i + 1) * LANES
                ]

    def mix_several(first_var, count, source):
        totals = [None] * count
        for k in range(3 * VARS):
            block = source[k]
            for i in range(count):
                term = block * star_rows[first_var + i, pl.ds(k, 1), :]
                totals[i] = term if totals[i] is None else totals[i] + term
        return totals

    def mix(left, emit):
        project(left, range(VARS), moved)

        def one_variable(p, carry):
            for i, values in enumerate(mix_several(3 * p, 3, moved)):
                emit(3 * p + i, values)
            return carry

        lax.fori_loop(0, VARS // 3, one_variable, 0)

    def weight(weights, degree):
        if isinstance(degree, int):
            return weights[degree]
        value = jnp.float32(weights[ORDER - 1])
        for k in range(ORDER - 2, 0, -1):
            value = jnp.where(degree == k, jnp.float32(weights[k]), value)
        return value

    def phase(step, carry):
        def begin(q):
            values = out[q]
            current[q] = right_operand(values, 8)
            half_sum[q] = values * half_weights[0]
            terms[0, q] = values

        def accumulate(chosen, group, begin, degree=None):
            totals = [None] * len(chosen)
            for q in group:
                for d in range(3):
                    block = (moved if q in lead else moved_rest)[d * VARS + q]
                    for i, p in enumerate(chosen):
                        term = block * star_rows[p, pl.ds(d * VARS + q, 1), :]
                        totals[i] = term if totals[i] is None else totals[i] + term
            for p, values in zip(chosen, totals):
                if not begin:
                    values = values + partial[p]
                if degree is None:
                    partial[p] = values
                else:
                    half_sum[p] += values * weight(half_weights, degree)
                    terms[degree, p] = values
                    current[p] = right_operand(values, 8)

        def first_part(degree):
            for chosen in [(0, 1, 2), (3, 4, 5), (6, 7, 8)]:
                accumulate(chosen, lead, True)
            project(left_derivative, rest, moved_rest)
            for chosen in [(0, 1, 2)]:
                accumulate(chosen, rest, False, degree)

        def finish(degree):
            for chosen in [(3, 4, 5), (6, 7, 8)]:
                accumulate(chosen, rest, False, degree)

        def turn_over(degree):
            if degree is not None:
                accumulate((3, 4, 5), rest, False, degree)
            project(left_derivative, lead, moved)
            if degree is not None:
                accumulate((6, 7, 8), rest, False, degree)

        def block(work):
            def once(i, carry):
                work()
                return carry

            lax.fori_loop(0, jnp.minimum(step + 1, 1), once, 0)

        def one_degree(degree, carry):
            block(lambda: first_part(degree))
            block(lambda: turn_over(degree))
            return carry

        for q in range(6):
            begin(q)
        turn_over(None)
        for q in range(6, VARS):
            begin(q)
        lax.fori_loop(1, ORDER - 1, one_degree, 0)
        block(lambda: first_part(ORDER - 1))
        finish(ORDER - 1)

        use_half = jnp.logical_or(cluster[...] == 1, step == 0)
        for q in range(VARS):
            current[q] = right_operand(jnp.where(use_half, half_sum[q], late_sum[q]), 8)

        right = jnp.concatenate([current[q] for q in range(VARS)], axis=1)
        projected = dot(left_restriction[...], right)
        for q in range(VARS):
            for f in range(4):
                tile = projected[f * FPAD : (f + 1) * FPAD, q * LANES : (q + 1) * LANES]
                own[f * VARS + q] = tile
                high, low = split(tile)
                lanes = pl.ds(f * LANES, LANES)
                candidates[pl.ds(q * FPAD, FPAD), lanes] = high.astype(BF16)
                candidates[pl.ds(WIDE + q * FPAD, FPAD), lanes] = low.astype(BF16)

        both = lax.dot_general(
            pick_send[pl.ds(0, GHOSTS), :],
            candidates[...],
            (((1,), (1,)), ((), ())),
            preferred_element_type=F32,
        )
        payload[step] = both[:, :WIDE] + both[:, WIDE:]
        if remote:

            @pl.when(step == 0)
            def _():
                pl.semaphore_wait(
                    barrier, n_sub - 1 + has_lower.astype(jnp.int32) + has_upper.astype(jnp.int32)
                )

            def transfer(i, peer, source, target, count):
                return pltpu.make_async_remote_copy(
                    src_ref=payload.at[step, pl.ds(source, count), :],
                    dst_ref=received.at[step, pl.ds(target, count), :],
                    send_sem=send_sem.at[step, i],
                    recv_sem=recv_sem.at[step, i],
                    device_id=peer,
                    device_id_type=MESH,
                )

            def to_lower():
                return transfer(0, lower, 0, CAP_DOM, CAP_DOM)

            def to_upper():
                return transfer(1, upper, CAP_DOM, 0, CAP_DOM)

            target = pl.multiple_of(2 * CAP_DOM + sub * CAP_SUB, CAP_SUB)
            copies = []
            for i, peer in enumerate(others):
                source = pl.multiple_of(2 * CAP_DOM + peer[1] * CAP_SUB, CAP_SUB)
                copies.append(transfer(2 + i, peer, source, target, CAP_SUB))
            pl.when(has_lower)(lambda: to_lower().start())
            pl.when(has_upper)(lambda: to_upper().start())
            for copy in copies:
                copy.start()
        mine = pl.multiple_of(2 * CAP_DOM + sub * CAP_SUB, CAP_SUB)
        received[step, pl.ds(mine, CAP_SUB), :] = payload[step, pl.ds(mine, CAP_SUB), :]

        @pl.when(step == 0)
        def _():
            rest_of_setup()

        def add_volume(p, values):
            out[p] += values

        mix(left_stiffness, add_volume)

        turn = lax.rem(flux[...], 3)

        def orient(values):
            for q in range(VARS):
                turned = dot(
                    left_orientation[...], right_operand(values[q * FPAD : (q + 1) * FPAD], 0)
                )
                for f in range(4):
                    lanes = slice(f * LANES, (f + 1) * LANES)
                    which = turn[f : f + 1]
                    other[f * VARS + q] = jnp.where(
                        which == 0,
                        turned[:FPAD, lanes],
                        jnp.where(
                            which == 1,
                            turned[FPAD : 2 * FPAD, lanes],
                            turned[2 * FPAD :, lanes],
                        ),
                    )

        def lift():
            right = jnp.concatenate([lift_in[p] for p in range(VARS)], axis=1)
            lifted = dot(left_lifting[...], right)
            for p in range(VARS):
                out[p] += lifted[:, p * LANES : (p + 1) * LANES]

        orient(
            dot(candidates[pl.ds(0, ROWS), :], pick_local[...])
            + dot(candidates[pl.ds(WIDE, ROWS), :], pick_local[...])
        )

        def both_sides(p, carry):
            tiles = []
            for f in range(4):
                total = None
                for q in range(VARS):
                    k = f * VARS + q
                    term = (
                        own[k] * minus_rows[p, pl.ds(k, 1), :]
                        + other[k] * plus_rows[p, pl.ds(k, 1), :]
                    )
                    total = term if total is None else total + term
                tiles.append(total)
            lift_in[p] = right_operand(jnp.concatenate(tiles, axis=0), 0)
            return carry

        lax.fori_loop(0, VARS, both_sides, 0)
        lift()

        if remote:
            for copy in copies:
                copy.wait()

            @pl.when(has_lower)
            def _():
                to_lower().wait_send()
                to_upper().wait_recv()

            @pl.when(has_upper)
            def _():
                to_upper().wait_send()
                to_lower().wait_recv()

        ghosts = jnp.transpose(received[step])
        turned = dot(
            left_orientation[...],
            jnp.concatenate(
                [right_operand(ghosts[q * FPAD : (q + 1) * FPAD], 0) for q in range(VARS)], axis=1
            ),
        )
        which = slot_turn[...]
        aligned = []
        for q in range(VARS):
            tile = turned[:, q * SLOTS : (q + 1) * SLOTS]
            aligned.append(
                jnp.where(
                    which == 0,
                    tile[:FPAD],
                    jnp.where(which == 1, tile[FPAD : 2 * FPAD], tile[2 * FPAD :]),
                )
            )
        for p in range(VARS):
            total = None
            for q in range(VARS):
                term = aligned[q] * slot_rows[p, pl.ds(q, 1), :]
                total = term if total is None else total + term
            high, low = split(total)
            mixed[pl.ds(p * FPAD, FPAD), pl.ds(0, SLOTS)] = high.astype(BF16)
            mixed[pl.ds(p * FPAD, FPAD), pl.ds(SLOTS, SLOTS)] = low.astype(BF16)
        scattered = dot(mixed[...], jnp.concatenate([pick_ghost[...]] * 2, axis=0))
        for p in range(VARS):
            tiles = [
                scattered[p * FPAD : (p + 1) * FPAD, f * LANES : (f + 1) * LANES] for f in range(4)
            ]
            lift_in[p] = right_operand(jnp.concatenate(tiles, axis=0), 0)
        lift()
        return carry

    lax.fori_loop(0, 2, phase, 0)


def body(
    modal_state,
    cluster_id,
    jacobian_id,
    face_neighbour,
    flux_index,
    send_list,
    derivative,
    stiffness,
    restriction,
    lifting,
    orientation,
    star_matrix,
    flux_minus,
    flux_plus,
    remote=True,
):
    n_dom, n_sub = (lax.axis_size("dom"), lax.axis_size("sub")) if remote else (1, 1)
    operands = (
        jnp.transpose(modal_state, (1, 0, 2)),
        cluster_id.reshape(1, LANES),
        jacobian_id.reshape(1, LANES),
        face_neighbour,
        flux_index,
        send_list.reshape(1, GHOSTS),
        derivative,
        stiffness,
        jnp.transpose(restriction, (1, 0, 2)),
        jnp.transpose(lifting, (2, 0, 1)),
        orientation,
        jnp.transpose(star_matrix, (2, 3, 1, 0)).reshape(PAIRS, 3, CLASSES),
        jnp.transpose(flux_minus, (2, 3, 1, 0)).reshape(PAIRS, 4, CLASSES),
        jnp.transpose(flux_plus, (2, 3, 1, 0)).reshape(PAIRS, 4, CLASSES),
    )
    operands = tuple(pltpu.with_memory_space_constraint(x, pltpu.HBM) for x in operands)
    n_peers = n_sub + 1
    result = pl.pallas_call(
        functools.partial(kernel, n_dom, n_sub, remote),
        name="elastic_step",
        out_shape=jax.ShapeDtypeStruct((VARS, BASIS, LANES), F32),
        in_specs=[pl.BlockSpec(memory_space=pltpu.HBM)] * len(operands),
        out_specs=pl.BlockSpec(memory_space=pltpu.VMEM),
        scratch_shapes=[
            pltpu.VMEM((PAIRS, 4, CLASSES) if x is operands[11] else x.shape, x.dtype)
            for x in operands[1:]
        ]
        + [
            pltpu.VMEM((4 * PAIRS, LANES), F32),
            pltpu.VMEM((VARS, 32, LANES), F32),
            pltpu.VMEM((VARS, 40, LANES), F32),
            pltpu.VMEM((VARS, 40, LANES), F32),
            pltpu.VMEM((3 * BASIS, KDIM), BF16),
            pltpu.VMEM((3 * BASIS, KDIM), BF16),
            pltpu.VMEM((4 * FPAD, KDIM), BF16),
            pltpu.VMEM((BASIS, 12 * FPAD), BF16),
            pltpu.VMEM((3 * FPAD, 3 * FPAD), BF16),
            pltpu.VMEM((4 * FPAD, BASIS), F32),
            pltpu.VMEM((3 * FPAD, FPAD), F32),
            pltpu.VMEM((SLOTS, 4 * LANES), BF16),
            pltpu.VMEM((4 * LANES, 4 * LANES), BF16),
            pltpu.VMEM((SLOTS, 4 * LANES), BF16),
            pltpu.VMEM((VARS, KDIM, LANES), BF16),
            pltpu.VMEM((3 * VARS, BASIS, LANES), F32),
            pltpu.VMEM((3 * VARS, BASIS, LANES), F32),
            pltpu.VMEM((VARS, BASIS, LANES), F32),
            pltpu.VMEM((VARS, BASIS, LANES), F32),
            pltpu.VMEM((VARS, BASIS, LANES), F32),
            pltpu.VMEM((ORDER, VARS, BASIS, LANES), F32),
            pltpu.VMEM((4 * VARS, FPAD, LANES), F32),
            pltpu.VMEM((4 * VARS, FPAD, LANES), F32),
            pltpu.VMEM((2 * WIDE, 4 * LANES), BF16),
            pltpu.VMEM((VARS, 12 * FPAD, LANES), BF16),
            pltpu.VMEM((ROWS, 2 * SLOTS), BF16),
            pltpu.VMEM((2, 4 * PAIRS, LANES), F32),
            pltpu.VMEM((VARS, 16, SLOTS), F32),
            pltpu.VMEM((1, SLOTS), jnp.int32),
            pltpu.VMEM((2, GHOSTS, WIDE), F32),
            pltpu.VMEM((2, SLOTS, WIDE), F32),
            pltpu.SemaphoreType.DMA((len(operands),)),
            pltpu.SemaphoreType.DMA((2, n_peers)),
            pltpu.SemaphoreType.DMA((2, n_peers)),
        ],
        compiler_params=pltpu.CompilerParams(
            collective_id=0 if remote else None,
            has_side_effects=True,
            vmem_limit_bytes=24 * 1024 * 1024,
        ),
    )(*operands)
    return jnp.transpose(result, (1, 0, 2))


def solution(mesh):
    placed = (
        P(None, None, ("dom", "sub")),
        P(("dom", "sub")),
        P(("dom", "sub")),
        P(None, ("dom", "sub")),
        P(None, ("dom", "sub")),
        P(("dom", "sub")),
        P(),
        P(),
        P(),
        P(),
        P(),
        P(),
        P(),
        P(),
    )
    return jax.shard_map(
        body, mesh=mesh, in_specs=placed, out_specs=P(None, None, ("dom", "sub")), check_vma=False
    )
```
